256 devices in a mesh: grp: 8 (over z_hi, core), mem: 32 (over z_lo, x, y).
Axes of the slice: x: 4, y: 4, z: 8 (z_hi: 4, z_lo: 2; z = z_hi * 2 + z_lo), core: 2. Of those that a mesh axis runs over, the one named last changes fastest.
Arguments:
- spectra: bfloat16 [2048, 2, 16, 512], P(('grp', 'mem')), may hold values from -40 to 40
- partners: int32 [2, 32], replicated, may hold values from 0 to 7, as said below
Outputs:
- correlations: bfloat16 [2048, 2, 256, 513], P(('grp', 'mem'))
The draws below stay inside these ranges and needn't reach their ends.
Inputs may be any that keep to these rules, and one draw needn't show every extreme that they name: For each member index k the offsets partners[r, k] of the rounds are distinct (offset 0 pairs a block with its own group).
All inputs are finite; a program needn't handle non-finite values.
Results may differ from the reference program's by a relative error of at most 0.0068.
Values may be sent and summed in bfloat16 or wider, within the bound.
No kernel may reach another device: no remote copies, remote signals or barrier semaphores. Data moves between devices by JAX's collectives and lax.ppermute only.
A program may use at most 128 MiB of HBM per device.

```python
import math
import jax
import jax.numpy as jnp
from jax import lax

CH_DEV = 8
SEG = 16
BINS = 512
SMOOTH = 32
LAGS = 513
GRP_CH = 256
NCH = 2048
R_WIN = 2
N_GRP = 8
N_MEM = 32


def draw_spectra(key, part):
    key_base = jax.random.fold_in(key, 11)
    key_level = jax.random.fold_in(key, 12)
    key_colour = jax.random.fold_in(key, 13)
    raw_values = jnp.clip(jax.random.normal(key_base, (NCH, 2, SEG, BINS), jnp.float32), -5.9, 5.9)
    loudness = jnp.exp(jax.random.uniform(key_level, (NCH, 1, SEG, 1), jnp.float32, -1.2, 1.2))
    colour = jnp.exp(jax.random.uniform(key_colour, (NCH, 1, 1, BINS), jnp.float32, -0.7, 0.7))
    return (raw_values * loudness * colour).astype(jnp.bfloat16)


def member_offsets(member_key):
    return jax.random.permutation(member_key, N_GRP)[:R_WIN].astype(jnp.int32)


def draw_partners(key, part):
    member_keys = jax.random.split(jax.random.fold_in(key, 21), N_MEM)
    table = jax.vmap(member_offsets)(member_keys)
    return jnp.transpose(table).astype(jnp.int32)


def setup_inputs(seed: int = 0) -> dict:
    key_list = jax.random.split(jax.random.key(seed), 3)
    spectra = draw_spectra(jax.random.fold_in(key_list[2], 71), 0)
    partners = draw_partners(jax.random.fold_in(key_list[2], 71), 0)
    return dict(spectra=spectra, partners=partners)


def whiten(spectra, half_width):
    components = spectra.astype(jnp.float32)
    power_sum = components[:, 0] * components[:, 0] + components[:, 1] * components[:, 1]
    bin_count = power_sum.shape[-1]
    positions = jnp.arange(bin_count, dtype=jnp.int32)
    band_matrix = (jnp.abs(positions[:, None] - positions[None, :]) <= half_width).astype(jnp.float32)
    smooth = jnp.dot(power_sum.reshape(-1, bin_count), band_matrix, precision=lax.Precision.HIGHEST)
    smooth = smooth.reshape(power_sum.shape) / (2 * half_width + 1)
    inv_level = lax.rsqrt(smooth + 1e-05)
    return (components * inv_level[:, None]).astype(jnp.bfloat16)

def lag_table(bin_count):
    centre = bin_count // 2
    frequency = jnp.arange(bin_count, dtype=jnp.int32)[:, None]
    lag_offset = jnp.arange(bin_count + 1, dtype=jnp.int32)[None, :] - centre
    angles = jnp.mod(frequency * lag_offset, 2 * bin_count).astype(jnp.float32) * (math.pi / bin_count)
    return jnp.stack([jnp.cos(angles), -jnp.sin(angles)], 0).astype(jnp.bfloat16)

def pair_lags(own_block, partner_block, transform):
    factor = math.sqrt(2.0 / (own_block.shape[3] * own_block.shape[2]))
    rotated = jnp.stack([own_block, jnp.stack([own_block[:, 1], -own_block[:, 0]], 1)], 0)
    cross_spectra = jnp.einsum('oicsf,jcsf->ofij', rotated.astype(jnp.float32), partner_block.astype(jnp.float32), precision=lax.Precision.HIGHEST).astype(jnp.bfloat16)
    lag_sums = jnp.einsum('ofij,ofl->ijl', cross_spectra.astype(jnp.float32), transform.astype(jnp.float32), precision=lax.Precision.HIGHEST)
    return (lag_sums * factor).astype(jnp.bfloat16)

def reference(spectra, partners):
    whitened = whiten(spectra, SMOOTH)
    transform = lag_table(BINS)
    blocks = whitened.reshape(N_GRP, GRP_CH, 2, SEG, BINS)
    column_index = jnp.arange(GRP_CH, dtype=jnp.int32)
    member_slot = column_index // CH_DEV
    per_round = []
    for round_index in range(R_WIN):
        slot_offsets = partners[round_index][member_slot].astype(jnp.int32)

        def one_group(group_index):
            own_block = lax.dynamic_index_in_dim(blocks, group_index, 0, keepdims=False)
            partner_rows = jnp.bitwise_xor(group_index, slot_offsets) * GRP_CH + column_index
            partner_block = jnp.take(whitened, partner_rows.astype(jnp.int32), axis=0)
            return pair_lags(own_block, partner_block, transform)
        result = lax.map(one_group, jnp.arange(N_GRP, dtype=jnp.int32))
        per_round.append(result.reshape(NCH, GRP_CH, LAGS))
    return jnp.stack(per_round, 1)
```

```python
import math

import jax
import jax.numpy as jnp
from jax import lax
from jax.experimental import pallas as pl
from jax.experimental.pallas import tpu as pltpu
from jax.sharding import PartitionSpec as P

SMOOTH = 32
CH = 8
COMP = 32
BINS = 512
LANE = 128
TAPS = BINS // LANE
LAGS = BINS + 1
LAG_ROWS = 520
PARAMS = pltpu.CompilerParams(vmem_limit_bytes=56 * 1024 * 1024)


def xor_perm(array, axis, mask):
    return lax.ppermute(array, axis, [(i, i ^ mask) for i in range(lax.axis_size(axis))])


def whiten_kernel(spectra_ref, out_ref, rows):
    comps = spectra_ref[...].astype(jnp.float32)
    power = (comps[:, 0] * comps[:, 0] + comps[:, 1] * comps[:, 1]).reshape(-1, BINS)
    row = lax.broadcasted_iota(jnp.int32, (BINS, BINS), 0)
    col = lax.broadcasted_iota(jnp.int32, (BINS, BINS), 1)
    band = (jnp.abs(row - col) <= SMOOTH).astype(jnp.float32)
    smooth = jnp.dot(
        power, band, precision=lax.Precision.HIGHEST, preferred_element_type=jnp.float32
    )
    inv = lax.rsqrt(smooth / (2 * SMOOTH + 1) + 1e-05)
    segs = COMP // 2
    for ch in range(CH):
        level = inv[ch * segs : (ch + 1) * segs]
        white = jnp.concatenate([comps[ch, 0] * level, comps[ch, 1] * level], 0)
        taps = jnp.concatenate([white[:, k * LANE : (k + 1) * LANE] for k in range(TAPS)], 0)
        rows[pl.ds(ch, LANE, stride=CH), :] = taps.T
    out_ref[...] = rows[...].reshape(LANE, CH, LANE).astype(jnp.bfloat16)


def whiten(spectra):
    return pl.pallas_call(
        whiten_kernel,
        out_shape=jax.ShapeDtypeStruct((LANE, CH, LANE), jnp.bfloat16),
        scratch_shapes=[pltpu.VMEM((LANE * CH, LANE), jnp.float32)],
        compiler_params=PARAMS,
        name="whiten",
    )(spectra)


def corr_kernel(factor, *refs):
    row_refs, col_refs, table_ref = refs[:4], refs[4:12], refs[12]
    out_refs, rows, cross = refs[13:17], refs[17], refs[18]
    lane = lax.broadcasted_iota(jnp.int32, (CH * LANE, LANE), 1)
    imag = lane // 16 % 2 == 1
    for d in range(4):
        own = row_refs[d][...].astype(jnp.float32).reshape(CH * LANE, LANE)
        rows[pl.ds(d * 1024, 1024), :] = own
        rows[pl.ds(4096 + d * 1024, 1024), :] = jnp.where(
            imag, -pltpu.roll(own, 16, 1), pltpu.roll(own, LANE - 16, 1)
        )
    sub = lax.broadcasted_iota(jnp.int32, (8, LANE), 0)
    tap = lax.broadcasted_iota(jnp.int32, (8, LANE), 1) // COMP
    pick_re = sub == tap
    pick_im = sub - TAPS == tap
    blank = jnp.zeros((64, LANE), jnp.bfloat16)

    def step(g, carry):
        cols = jnp.concatenate([c[g].astype(jnp.float32) for c in col_refs], 0).astype(jnp.bfloat16)
        rhs = jnp.concatenate(
            [jnp.concatenate([cols, blank], 1), jnp.concatenate([blank, cols], 1)], 0
        )
        pairs = []
        for pair in range(16):
            halves = []
            for half in range(2):
                i = 2 * pair + half
                at = (i // 8) * 1024 + g * 8 + i % 8
                re = jnp.broadcast_to(rows[pl.ds(at, 1), :], (8, LANE))
                im = jnp.broadcast_to(rows[pl.ds(4096 + at, 1), :], (8, LANE))
                halves.append(jnp.where(pick_re, re, jnp.where(pick_im, im, 0.0)))
            pairs.append(jnp.concatenate(halves, 1))
        lhs = jnp.concatenate(pairs, 0).astype(jnp.bfloat16)
        prod = lax.dot_general(
            lhs, rhs, (((1,), (1,)), ((), ())), preferred_element_type=jnp.float32
        )
        at = pl.multiple_of(g * 8, 8)
        for pair in range(16):
            cross[pair, pl.ds(at, 8), :] = prod[pair * 8 : pair * 8 + 8]
        return carry

    lax.fori_loop(0, LANE, step, 0)
    table = table_ref[...]
    for d in range(4):
        for quad in range(2):
            pair = d * 4 + quad * 2
            weights = jnp.concatenate([cross[pair], cross[pair + 1]], 1).astype(jnp.bfloat16)
            lags = jnp.dot(table, weights, preferred_element_type=jnp.float32)
            out_refs[d][quad] = (lags * factor).astype(jnp.bfloat16)


def correlate(row_blocks, col_blocks, table, factor):
    def body(*refs):
        corr_kernel(factor, *refs)

    return pl.pallas_call(
        body,
        out_shape=[jax.ShapeDtypeStruct((2, LAG_ROWS, 256), jnp.bfloat16)] * 4,
        scratch_shapes=[
            pltpu.VMEM((8 * 1024, LANE), jnp.float32),
            pltpu.VMEM((16, 1024, LANE), jnp.float32),
        ],
        compiler_params=PARAMS,
        name="correlate",
    )(*row_blocks, *col_blocks, table)


def finish_kernel(*refs):
    parts, order_ref, out_ref, buf = refs[:8], refs[8], refs[9], refs[10]
    for i2 in range(4):
        for half in range(2):
            i = i2 * 2 + half
            quad, at = i // 4, (i // 2) % 2 * LANE
            for r in range(2):
                wide = jnp.concatenate(
                    [parts[r * 4 + d][quad, :, at : at + LANE] for d in range(4)], 1
                )
                ordered = jnp.dot(wide, order_ref[r, half], preferred_element_type=jnp.float32)
                for tile in range(2):
                    buf[pl.ds(half * 4 * LAGS + tile * 2 + r, LAGS, stride=4), :] = ordered[
                        :LAGS, tile * LANE : (tile + 1) * LANE
                    ]
        out_ref[i2] = buf[...].astype(jnp.bfloat16)


def finish(parts, order):
    return pl.pallas_call(
        finish_kernel,
        out_shape=jax.ShapeDtypeStruct((4, 8 * LAGS, LANE), jnp.bfloat16),
        scratch_shapes=[pltpu.VMEM((8 * LAGS, LANE), jnp.float32)],
        compiler_params=PARAMS,
        name="finish",
    )(*parts, order)


def lag_table():
    lag = jnp.arange(LAG_ROWS, dtype=jnp.int32)[:, None]
    k = jnp.arange(2 * BINS, dtype=jnp.int32)[None, :]
    frequency = k % TAPS * LANE + k // 8
    angles = jnp.mod(frequency * (lag - BINS // 2), 2 * BINS).astype(jnp.float32) * (math.pi / BINS)
    values = jnp.where(k // TAPS % 2 == 0, jnp.cos(angles), -jnp.sin(angles))
    return jnp.where(lag < LAGS, values, 0.0).astype(jnp.bfloat16)


def column_order(member):
    z, x, y = member // 16, member // 4 % 4, member % 4
    at = jnp.arange(512, dtype=jnp.int32)
    d, half, block, ch = at // 128, at // 64 % 2, at // 8 % 8, at % 8
    ez, e = block // 4, block % 4
    first = (z ^ ez) * 128 + (x ^ d) * 32 + (y ^ e) * 8 + ch
    second = (z ^ ez) * 128 + (x ^ e) * 32 + (y ^ d) * 8 + ch
    target = jnp.stack([first, second], 0)[:, None, :, None]
    column = jnp.arange(256, dtype=jnp.int32)[None, None, None, :]
    side = jnp.arange(2, dtype=jnp.int32)[None, :, None, None]
    return ((target == column) & (half[None, None, :, None] == side)).astype(jnp.bfloat16)


def on_device(spectra, partners):
    member = lax.axis_index("mem").astype(jnp.int32)
    white = whiten(spectra)
    planes = [white] + [xor_perm(white, "grp", 2 * d) for d in range(1, 4)]
    row_masks, col_masks = (4, 1), (1, 4)
    rows = [[white] + [xor_perm(white, "mem", d * m) for d in range(1, 4)] for m in row_masks]
    table = lag_table()
    order = column_order(member)
    factor = math.sqrt(2.0 / (BINS * (COMP // 2)))
    cols = []
    for r in range(2):
        offset = partners[r, member]
        plane = offset >> 1
        mine = jnp.where(
            plane == 0,
            planes[0],
            jnp.where(plane == 1, planes[1], jnp.where(plane == 2, planes[2], planes[3])),
        )
        other = xor_perm(mine, "grp", 1)
        block = jnp.where((offset & 1) == 1, other, mine)
        far = xor_perm(block, "mem", 16)
        cols.append(
            [block]
            + [xor_perm(block, "mem", e * col_masks[r]) for e in range(1, 4)]
            + [far]
            + [xor_perm(far, "mem", e * col_masks[r]) for e in range(1, 4)]
        )
    parts = []
    for r in range(2):
        sums = correlate(rows[r], cols[r], table, factor)
        parts += [sums[0]] + [xor_perm(sums[d], "mem", d * row_masks[r]) for d in range(1, 4)]
    packed = finish(parts, order)
    result = packed.reshape(CH, LAGS, 2, 2, LANE)
    return jnp.transpose(result, (0, 3, 2, 4, 1)).reshape(CH, 2, 256, LAGS)


def solution(mesh):
    placed = (P(("grp", "mem"), None, None, None), P())
    return jax.shard_map(
        on_device,
        mesh=mesh,
        in_specs=placed,
        out_specs=P(("grp", "mem"), None, None, None),
        check_vma=False,
    )
```

```python
import math

import jax
import jax.numpy as jnp
from jax import lax
from jax.experimental import pallas as pl
from jax.experimental.pallas import tpu as pltpu
from jax.sharding import PartitionSpec as P

SMOOTH = 32
CH = 8
COMP = 32
BINS = 512
LANE = 128
TAPS = BINS // LANE
LAGS = BINS + 1
LAG_ROWS = 520
UNROLL = 16


def vmem(mib):
    return pltpu.CompilerParams(vmem_limit_bytes=mib * 1024 * 1024)


def xor_perm(array, axis, mask):
    return lax.ppermute(array, axis, [(i, i ^ mask) for i in range(lax.axis_size(axis))])


def whiten_kernel(spectra_ref, out_ref, rows):
    comps = spectra_ref[...].astype(jnp.float32)
    power = (comps[:, 0] * comps[:, 0] + comps[:, 1] * comps[:, 1]).reshape(-1, BINS)
    row = lax.broadcasted_iota(jnp.int32, (BINS, BINS), 0)
    col = lax.broadcasted_iota(jnp.int32, (BINS, BINS), 1)
    band = (jnp.abs(row - col) <= SMOOTH).astype(jnp.float32)
    smooth = jnp.dot(
        power, band, precision=lax.Precision.HIGHEST, preferred_element_type=jnp.float32
    )
    inv = lax.rsqrt(smooth / (2 * SMOOTH + 1) + 1e-05)
    segs = COMP // 2
    for ch in range(CH):
        level = inv[ch * segs : (ch + 1) * segs]
        white = jnp.concatenate([comps[ch, 0] * level, comps[ch, 1] * level], 0)
        taps = jnp.concatenate([white[:, k * LANE : (k + 1) * LANE] for k in range(TAPS)], 0)
        rows[pl.ds(ch, LANE, stride=CH), :] = taps.T
    out_ref[...] = rows[...].reshape(LANE, CH, LANE).astype(jnp.bfloat16)


def whiten(spectra):
    return pl.pallas_call(
        whiten_kernel,
        out_shape=jax.ShapeDtypeStruct((LANE, CH, LANE), jnp.bfloat16),
        scratch_shapes=[pltpu.VMEM((LANE * CH, LANE), jnp.float32)],
        compiler_params=vmem(12),
        name="whiten",
    )(spectra)


def corr_kernel(factor, *refs):
    row_refs, col_refs, table_ref = refs[:4], refs[4:12], refs[12]
    out_refs, rows, cross = refs[13:17], refs[17], refs[18]
    lane = lax.broadcasted_iota(jnp.int32, (CH * LANE, LANE), 1)
    imag = lane // 16 % 2 == 1
    for d in range(4):
        own = row_refs[d][...].astype(jnp.float32).reshape(CH * LANE, LANE)
        rows[pl.ds(d * 1024, 1024), :] = own
        rows[pl.ds(4096 + d * 1024, 1024), :] = jnp.where(
            imag, -pltpu.roll(own, 16, 1), pltpu.roll(own, LANE - 16, 1)
        )
    sub = lax.broadcasted_iota(jnp.int32, (8, LANE), 0)
    tap = lax.broadcasted_iota(jnp.int32, (8, LANE), 1) // COMP
    pick_re = sub == tap
    pick_im = sub - TAPS == tap
    blank = jnp.zeros((64, LANE), jnp.bfloat16)

    def step(g):
        cols = jnp.concatenate([c[g].astype(jnp.float32) for c in col_refs], 0).astype(jnp.bfloat16)
        rhs = jnp.concatenate(
            [jnp.concatenate([cols, blank], 1), jnp.concatenate([blank, cols], 1)], 0
        )
        pairs = []
        for pair in range(16):
            halves = []
            for half in range(2):
                i = 2 * pair + half
                at = (i // 8) * 1024 + g * 8 + i % 8
                re = rows[pl.ds(at, 8, stride=0), :]
                im = rows[pl.ds(4096 + at, 8, stride=0), :]
                halves.append(jnp.where(pick_re, re, jnp.where(pick_im, im, 0.0)))
            pairs.append(jnp.concatenate(halves, 1))
        lhs = jnp.concatenate(pairs, 0).astype(jnp.bfloat16)
        prod = lax.dot_general(
            lhs, rhs, (((1,), (1,)), ((), ())), preferred_element_type=jnp.float32
        )
        at = pl.multiple_of(g * 8, 8)
        for pair in range(16):
            cross[pair, pl.ds(at, 8), :] = prod[pair * 8 : pair * 8 + 8]

    def steps(k, carry):
        for u in range(UNROLL):
            step(k * UNROLL + u)
        return carry

    lax.fori_loop(0, LANE // UNROLL, steps, 0)
    table = table_ref[...]
    for d in range(4):
        for quad in range(2):
            pair = d * 4 + quad * 2
            weights = jnp.concatenate([cross[pair], cross[pair + 1]], 1).astype(jnp.bfloat16)
            lags = jnp.dot(table, weights, preferred_element_type=jnp.float32)
            out_refs[d][quad] = (lags * factor).astype(jnp.bfloat16)


def correlate(row_blocks, col_blocks, table, factor):
    def body(*refs):
        corr_kernel(factor, *refs)

    return pl.pallas_call(
        body,
        out_shape=[jax.ShapeDtypeStruct((2, LAG_ROWS, 256), jnp.bfloat16)] * 4,
        scratch_shapes=[
            pltpu.VMEM((8 * 1024, LANE), jnp.float32),
            pltpu.VMEM((16, 1024, LANE), jnp.float32),
        ],
        compiler_params=vmem(30),
        name="correlate",
    )(*row_blocks, *col_blocks, table)


def finish_kernel(*refs):
    parts, order_ref, out_ref, buf = refs[:8], refs[8], refs[9], refs[10]
    for i2 in range(4):
        for half in range(2):
            i = i2 * 2 + half
            quad, at = i // 4, (i // 2) % 2 * LANE
            for r in range(2):
                wide = jnp.concatenate(
                    [parts[r * 4 + d][quad, :, at : at + LANE] for d in range(4)], 1
                )
                ordered = jnp.dot(wide, order_ref[r, half], preferred_element_type=jnp.float32)
                for tile in range(2):
                    buf[pl.ds(half * 4 * LAGS + tile * 2 + r, LAGS, stride=4), :] = ordered[
                        :LAGS, tile * LANE : (tile + 1) * LANE
                    ]
        out_ref[i2] = buf[...].astype(jnp.bfloat16)


def finish(parts, order):
    return pl.pallas_call(
        finish_kernel,
        out_shape=jax.ShapeDtypeStruct((4, 8 * LAGS, LANE), jnp.bfloat16),
        scratch_shapes=[pltpu.VMEM((8 * LAGS, LANE), jnp.float32)],
        compiler_params=vmem(24),
        name="finish",
    )(*parts, order)


def lag_table():
    lag = jnp.arange(LAG_ROWS, dtype=jnp.int32)[:, None]
    k = jnp.arange(2 * BINS, dtype=jnp.int32)[None, :]
    frequency = k % TAPS * LANE + k // 8
    angles = jnp.mod(frequency * (lag - BINS // 2), 2 * BINS).astype(jnp.float32) * (math.pi / BINS)
    values = jnp.where(k // TAPS % 2 == 0, jnp.cos(angles), -jnp.sin(angles))
    return jnp.where(lag < LAGS, values, 0.0).astype(jnp.bfloat16)


def column_order(member):
    z, x, y = member // 16, member // 4 % 4, member % 4
    at = jnp.arange(512, dtype=jnp.int32)
    d, half, block, ch = at // 128, at // 64 % 2, at // 8 % 8, at % 8
    ez, e = block // 4, block % 4
    first = (z ^ ez) * 128 + (x ^ d) * 32 + (y ^ e) * 8 + ch
    second = (z ^ ez) * 128 + (x ^ e) * 32 + (y ^ d) * 8 + ch
    target = jnp.stack([first, second], 0)[:, None, :, None]
    column = jnp.arange(256, dtype=jnp.int32)[None, None, None, :]
    side = jnp.arange(2, dtype=jnp.int32)[None, :, None, None]
    return ((target == column) & (half[None, None, :, None] == side)).astype(jnp.bfloat16)


def on_device(spectra, partners):
    member = lax.axis_index("mem").astype(jnp.int32)
    white = whiten(spectra)
    planes = [white] + [xor_perm(white, "grp", 2 * d) for d in range(1, 4)]
    row_masks, col_masks = (4, 1), (1, 4)
    order = column_order(member)
    source, order = lax.optimization_barrier((white, order))
    rows = [[white, None, None, None], [white, None, None, None]]
    for d in (1, 3, 2):
        sent = [xor_perm(source, "mem", d * m) for m in row_masks]
        source, sent = lax.optimization_barrier((source, sent))
        rows[0][d], rows[1][d] = sent
    table = lag_table()
    factor = math.sqrt(2.0 / (BINS * (COMP // 2)))
    planes, rows, table, order = lax.optimization_barrier((planes, rows, table, order))
    mine = []
    for r in range(2):
        plane = partners[r, member] >> 1
        mine.append(
            jnp.where(
                plane == 0,
                planes[0],
                jnp.where(plane == 1, planes[1], jnp.where(plane == 2, planes[2], planes[3])),
            )
        )
    other = [xor_perm(m, "grp", 1) for m in mine]
    near = [jnp.where((partners[r, member] & 1) == 1, other[r], mine[r]) for r in range(2)]
    far = [xor_perm(b, "mem", 16) for b in near]
    cols = [[None] * 8, [None] * 8]
    sent = [[], []]
    for block, sources in ((0, near), (4, far)):
        for r in range(2):
            cols[r][block] = sources[r]
        for e in (1, 3, 2):
            for r in range(2):
                source = sources[r]
                if len(sent[r]) >= 2:
                    source, _ = lax.optimization_barrier((source, sent[r][-2]))
                cols[r][block + e] = xor_perm(source, "mem", e * col_masks[r])
                sent[r].append(cols[r][block + e])
    cols = lax.optimization_barrier(cols)
    parts = []
    for r in range(2):
        sums = correlate(rows[r], cols[r], table, factor)
        parts += [sums[0]] + [xor_perm(sums[d], "mem", d * row_masks[r]) for d in range(1, 4)]
    packed = finish(parts, order)
    result = packed.reshape(CH, LAGS, 2, 2, LANE)
    return jnp.transpose(result, (0, 3, 2, 4, 1)).reshape(CH, 2, 256, LAGS)


def solution(mesh):
    placed = (P(("grp", "mem"), None, None, None), P())
    return jax.shard_map(
        on_device,
        mesh=mesh,
        in_specs=placed,
        out_specs=P(("grp", "mem"), None, None, None),
        check_vma=False,
    )
```

```python
import math

import jax
import jax.numpy as jnp
from jax import lax
from jax.experimental import pallas as pl
from jax.experimental.pallas import tpu as pltpu
from jax.sharding import PartitionSpec as P

SMOOTH = 32
CH = 8
COMP = 32
BINS = 512
LANE = 128
TAPS = BINS // LANE
LAGS = BINS + 1
LAG_ROWS = 520
UNROLL = 16


def vmem(mib):
    return pltpu.CompilerParams(vmem_limit_bytes=mib * 1024 * 1024)


def xor_perm(array, axis, mask):
    return lax.ppermute(array, axis, [(i, i ^ mask) for i in range(lax.axis_size(axis))])


def whiten_kernel(spectra_ref, out_ref, rows):
    comps = spectra_ref[...].astype(jnp.float32)
    power = (comps[:, 0] * comps[:, 0] + comps[:, 1] * comps[:, 1]).reshape(-1, BINS)
    row = lax.broadcasted_iota(jnp.int32, (BINS, BINS), 0)
    col = lax.broadcasted_iota(jnp.int32, (BINS, BINS), 1)
    band = (jnp.abs(row - col) <= SMOOTH).astype(jnp.float32)
    smooth = jnp.dot(
        power, band, precision=lax.Precision.HIGHEST, preferred_element_type=jnp.float32
    )
    inv = lax.rsqrt(smooth / (2 * SMOOTH + 1) + 1e-05)
    segs = COMP // 2
    for ch in range(CH):
        level = inv[ch * segs : (ch + 1) * segs]
        white = jnp.concatenate([comps[ch, 0] * level, comps[ch, 1] * level], 0)
        taps = jnp.concatenate([white[:, k * LANE : (k + 1) * LANE] for k in range(TAPS)], 0)
        rows[pl.ds(ch, LANE, stride=CH), :] = taps.T
    out_ref[...] = rows[...].reshape(LANE, CH, LANE).astype(jnp.bfloat16)


def whiten(spectra):
    return pl.pallas_call(
        whiten_kernel,
        out_shape=jax.ShapeDtypeStruct((LANE, CH, LANE), jnp.bfloat16),
        scratch_shapes=[pltpu.VMEM((LANE * CH, LANE), jnp.float32)],
        compiler_params=vmem(10),
        name="whiten",
    )(spectra)


def pick_kernel(member_ref, partners_ref, *refs):
    planes, out_ref = refs[:4], refs[4]
    for r in range(2):
        distance = partners_ref[r, member_ref[0]] >> 1
        for d in range(4):

            @pl.when(distance == d)
            def _():
                out_ref[r] = planes[d][...]


def merge_kernel(member_ref, partners_ref, mine_ref, other_ref, out_ref):
    for r in range(2):
        swap = partners_ref[r, member_ref[0]] & 1

        @pl.when(swap == 1)
        def _():
            out_ref[r] = other_ref[r]

        @pl.when(swap == 0)
        def _():
            out_ref[r] = mine_ref[r]


def choose(kernel, name, member, partners, arrays):
    smem, whole = pl.BlockSpec(memory_space=pltpu.SMEM), pl.BlockSpec(memory_space=pltpu.VMEM)
    return pl.pallas_call(
        kernel,
        in_specs=[smem, smem] + [whole] * len(arrays),
        out_shape=jax.ShapeDtypeStruct((2, LANE, CH, LANE), jnp.bfloat16),
        compiler_params=vmem(10),
        name=name,
    )(member, partners, *arrays)


def corr_kernel(factor, *refs):
    row_refs, col_refs, table_ref = refs[:4], refs[4:8], refs[8]
    out_refs, rows, cross = refs[9:13], refs[13], refs[14]
    lane = lax.broadcasted_iota(jnp.int32, (CH * LANE, LANE), 1)
    imag = lane // 16 % 2 == 1
    for d in range(4):
        own = row_refs[d][...].astype(jnp.float32).reshape(CH * LANE, LANE)
        rows[pl.ds(d * 1024, 1024), :] = own
        rows[pl.ds(4096 + d * 1024, 1024), :] = jnp.where(
            imag, -pltpu.roll(own, 16, 1), pltpu.roll(own, LANE - 16, 1)
        )
    sub = lax.broadcasted_iota(jnp.int32, (8, LANE), 0)
    tap = lax.broadcasted_iota(jnp.int32, (8, LANE), 1) // COMP
    pick_re = sub == tap
    pick_im = sub - TAPS == tap
    blank = jnp.zeros((64, LANE), jnp.bfloat16)

    def step(g):
        cols = jnp.concatenate(
            [c[n, g].astype(jnp.float32) for c in col_refs for n in range(2)], 0
        ).astype(jnp.bfloat16)
        rhs = jnp.concatenate(
            [jnp.concatenate([cols, blank], 1), jnp.concatenate([blank, cols], 1)], 0
        )
        pairs = []
        for pair in range(16):
            halves = []
            for half in range(2):
                i = 2 * pair + half
                at = (i // 8) * 1024 + g * 8 + i % 8
                re = rows[pl.ds(at, 8, stride=0), :]
                im = rows[pl.ds(4096 + at, 8, stride=0), :]
                halves.append(jnp.where(pick_re, re, jnp.where(pick_im, im, 0.0)))
            pairs.append(jnp.concatenate(halves, 1))
        lhs = jnp.concatenate(pairs, 0).astype(jnp.bfloat16)
        prod = lax.dot_general(
            lhs, rhs, (((1,), (1,)), ((), ())), preferred_element_type=jnp.float32
        )
        at = pl.multiple_of(g * 8, 8)
        for pair in range(16):
            cross[pair, pl.ds(at, 8), :] = prod[pair * 8 : pair * 8 + 8]

    def steps(k, carry):
        for u in range(UNROLL):
            step(k * UNROLL + u)
        return carry

    lax.fori_loop(0, LANE // UNROLL, steps, 0)
    table = table_ref[...]
    for d in range(4):
        for quad in range(2):
            pair = d * 4 + quad * 2
            weights = jnp.concatenate([cross[pair], cross[pair + 1]], 1).astype(jnp.bfloat16)
            lags = jnp.dot(table, weights, preferred_element_type=jnp.float32)
            out_refs[d][quad] = (lags * factor).astype(jnp.bfloat16)


def correlate(row_blocks, col_blocks, table, factor):
    def body(*refs):
        corr_kernel(factor, *refs)

    return pl.pallas_call(
        body,
        out_shape=[jax.ShapeDtypeStruct((2, LAG_ROWS, 256), jnp.bfloat16)] * 4,
        scratch_shapes=[
            pltpu.VMEM((8 * 1024, LANE), jnp.float32),
            pltpu.VMEM((16, 1024, LANE), jnp.float32),
        ],
        compiler_params=vmem(24),
        cost_estimate=pl.CostEstimate(
            flops=2 * LANE * LANE * 256 * LANE + 16 * LAG_ROWS * 1024 * 256,
            transcendentals=0,
            bytes_accessed=7 * 1024 * 1024,
        ),
        name="correlate",
    )(*row_blocks, *col_blocks, table)


def finish_kernel(*refs):
    parts, order_ref, out_ref, buf = refs[:8], refs[8], refs[9], refs[10]
    for i2 in range(4):
        for half in range(2):
            i = i2 * 2 + half
            quad, at = i // 4, (i // 2) % 2 * LANE
            wide = jnp.concatenate([p[quad, :, at : at + LANE] for p in parts], 1)
            for r in range(2):
                ordered = jnp.dot(wide, order_ref[r, half], preferred_element_type=jnp.float32)
                for tile in range(2):
                    buf[pl.ds(half * 4 * LAGS + tile * 2 + r, LAGS, stride=4), :] = ordered[
                        :LAGS, tile * LANE : (tile + 1) * LANE
                    ]
        out_ref[i2] = buf[...].astype(jnp.bfloat16)


def finish(parts, order):
    return pl.pallas_call(
        finish_kernel,
        out_shape=jax.ShapeDtypeStruct((4, 8 * LAGS, LANE), jnp.bfloat16),
        scratch_shapes=[pltpu.VMEM((8 * LAGS, LANE), jnp.float32)],
        compiler_params=vmem(18),
        name="finish",
    )(*parts, order)


def lag_table():
    lag = jnp.arange(LAG_ROWS, dtype=jnp.int32)[:, None]
    k = jnp.arange(2 * BINS, dtype=jnp.int32)[None, :]
    frequency = k % TAPS * LANE + k // 8
    n = frequency * (lag - BINS // 2) + k // TAPS % 2 * (BINS // 2)
    turn = (n + BINS // 4) // (BINS // 2)
    x = (n - turn * (BINS // 2)).astype(jnp.float32) * (math.pi / BINS)
    x2 = x * x
    cos, sin = jnp.float32(0), jnp.float32(0)
    for power in range(10, -1, -2):
        cos = cos * x2 + (-1) ** (power // 2) / math.factorial(power)
        sin = sin * x2 + (-1) ** (power // 2) / math.factorial(power + 1)
    values = jnp.where(turn % 2 == 0, cos, sin * x)
    values = jnp.where((turn + 1) // 2 % 2 == 0, values, -values)
    return jnp.where(lag < LAGS, values, 0.0).astype(jnp.bfloat16)


def column_order(member):
    z, x, y = member // 16, member // 4 % 4, member % 4
    at = jnp.arange(1024, dtype=jnp.int32)
    far, d, half, e, turn, ch = at // 512, at // 128 % 4, at // 64 % 2, at // 16 % 4, at // 8 % 2, at % 8
    dx, dy = jnp.where(far == 1, e, d), jnp.where(far == 1, d, e)
    target = (z ^ far) * 128 + (x ^ dx) * 32 + (y ^ dy) * 8 + ch
    target = target + 256 * half + 512 * turn
    column = jnp.arange(256, dtype=jnp.int32)[None, None, None, :]
    side = jnp.arange(2, dtype=jnp.int32)[None, :, None, None]
    turns = jnp.arange(2, dtype=jnp.int32)[:, None, None, None]
    return (target[None, None, :, None] == column + 256 * side + 512 * turns).astype(jnp.bfloat16)


def on_device(spectra, partners):
    member = lax.axis_index("mem").astype(jnp.int32)
    white = whiten(spectra)
    row_masks, col_masks = (4, 1), (1, 4)
    rows = [[white, None, None, None], [white, None, None, None]]
    source = white
    for d in (1, 3, 2):
        sent = [xor_perm(source, "mem", d * m) for m in row_masks]
        source, sent = lax.optimization_barrier((source, sent))
        rows[0][d], rows[1][d] = sent
    planes = [white] + [xor_perm(white, "grp", 2 * d) for d in range(1, 4)]
    table = lag_table()
    order = column_order(member)
    factor = math.sqrt(2.0 / (BINS * (COMP // 2)))
    planes, rows, table, order = lax.optimization_barrier((planes, rows, table, order))

    mine = choose(pick_kernel, "pick", member.reshape(1), partners, planes)
    other = xor_perm(mine, "grp", 1)
    near = choose(merge_kernel, "merge", member.reshape(1), partners, [mine, other])
    across = xor_perm(near, "mem", 16)
    cols = [[near, None, None, None], [across, None, None, None]]
    for e in (3, 1):
        cols[0][e] = xor_perm(near, "mem", e * col_masks[0])
    cols, near, across = lax.optimization_barrier((cols, near, across))
    for e in (3, 1):
        cols[1][e] = xor_perm(across, "mem", e * col_masks[1])
    cols[0][2] = xor_perm(near, "mem", 2 * col_masks[0])
    cols, across = lax.optimization_barrier((cols, across))
    cols[1][2] = xor_perm(across, "mem", 2 * col_masks[1])
    parts = []
    for n in range(2):
        sums = correlate(rows[n], cols[n], table, factor)
        parts += [sums[0]] + [xor_perm(sums[d], "mem", d * row_masks[n]) for d in range(1, 4)]
        cols[1], sums = lax.optimization_barrier((cols[1], sums[0]))
    packed = finish(parts, order)
    result = packed.reshape(CH, LAGS, 2, 2, LANE)
    return jnp.transpose(result, (0, 3, 2, 4, 1)).reshape(CH, 2, 256, LAGS)


def solution(mesh):
    placed = (P(("grp", "mem"), None, None, None), P())
    return jax.shard_map(
        on_device,
        mesh=mesh,
        in_specs=placed,
        out_specs=P(("grp", "mem"), None, None, None),
        check_vma=False,
    )
```

```python
import math

import jax
import jax.numpy as jnp
from jax import lax
from jax.experimental import pallas as pl
from jax.experimental.pallas import tpu as pltpu
from jax.sharding import PartitionSpec as P

SMOOTH = 32
CH = 8
COMP = 32
BINS = 512
LANE = 128
TAPS = BINS // LANE
LAGS = BINS + 1
LAG_ROWS = 520
UNROLL = 16


def vmem(mib):
    return pltpu.CompilerParams(vmem_limit_bytes=mib * 1024 * 1024)


def xor_perm(array, axis, mask):
    return lax.ppermute(array, axis, [(i, i ^ mask) for i in range(lax.axis_size(axis))])


def ring_perm(array, shift):
    size = lax.axis_size("grp")
    return lax.ppermute(array, "grp", [(i, (i + 2 * shift) % size) for i in range(size)])


def whiten_kernel(spectra_ref, out_ref, rows):
    comps = spectra_ref[...].astype(jnp.float32)
    power = (comps[:, 0] * comps[:, 0] + comps[:, 1] * comps[:, 1]).reshape(-1, BINS)
    row = lax.broadcasted_iota(jnp.int32, (BINS, BINS), 0)
    col = lax.broadcasted_iota(jnp.int32, (BINS, BINS), 1)
    band = (jnp.abs(row - col) <= SMOOTH).astype(jnp.float32)
    smooth = jnp.dot(
        power, band, precision=lax.Precision.HIGHEST, preferred_element_type=jnp.float32
    )
    inv = lax.rsqrt(smooth / (2 * SMOOTH + 1) + 1e-05)
    segs = COMP // 2
    for ch in range(CH):
        level = inv[ch * segs : (ch + 1) * segs]
        white = jnp.concatenate([comps[ch, 0] * level, comps[ch, 1] * level], 0)
        taps = jnp.concatenate([white[:, k * LANE : (k + 1) * LANE] for k in range(TAPS)], 0)
        rows[pl.ds(ch, LANE, stride=CH), :] = taps.T
    out_ref[...] = rows[...].reshape(LANE, CH, LANE).astype(jnp.bfloat16)


def whiten(spectra):
    return pl.pallas_call(
        whiten_kernel,
        out_shape=jax.ShapeDtypeStruct((LANE, CH, LANE), jnp.bfloat16),
        scratch_shapes=[pltpu.VMEM((LANE * CH, LANE), jnp.float32)],
        compiler_params=vmem(10),
        name="whiten",
    )(spectra)


def pick_kernel(where_ref, partners_ref, *refs):
    blocks, tops, out_ref = refs[:3], refs[3:5], refs[5]
    here = where_ref[1]
    for r in range(2):
        shift = ((here ^ (partners_ref[r, where_ref[0]] >> 1)) - here) & 3
        for s in range(4):

            @pl.when(shift == s)
            def _():
                if s == 2:
                    out_ref[r, : LANE // 2] = tops[0][...]
                    out_ref[r, LANE // 2 :] = tops[1][...]
                else:
                    out_ref[r] = blocks[s - (s > 2)][...]


def merge_kernel(where_ref, partners_ref, mine_ref, other_ref, out_ref):
    for r in range(2):
        swap = partners_ref[r, where_ref[0]] & 1

        @pl.when(swap == 1)
        def _():
            out_ref[r] = other_ref[r]

        @pl.when(swap == 0)
        def _():
            out_ref[r] = mine_ref[r]


def choose(kernel, name, where, partners, arrays):
    smem, whole = pl.BlockSpec(memory_space=pltpu.SMEM), pl.BlockSpec(memory_space=pltpu.VMEM)
    return pl.pallas_call(
        kernel,
        in_specs=[smem, smem] + [whole] * len(arrays),
        out_shape=jax.ShapeDtypeStruct((2, LANE, CH, LANE), jnp.bfloat16),
        compiler_params=vmem(10),
        name=name,
    )(where, partners, *arrays)


def corr_kernel(factor, *refs):
    row_refs, col_refs, table_ref = refs[:4], refs[4:8], refs[8]
    out_refs, rows, cross = refs[9:13], refs[13], refs[14]
    lane = lax.broadcasted_iota(jnp.int32, (CH * LANE, LANE), 1)
    imag = lane // 16 % 2 == 1
    for d in range(4):
        own = row_refs[d][...].astype(jnp.float32).reshape(CH * LANE, LANE)
        rows[pl.ds(d * 1024, 1024), :] = own
        rows[pl.ds(4096 + d * 1024, 1024), :] = jnp.where(
            imag, -pltpu.roll(own, 16, 1), pltpu.roll(own, LANE - 16, 1)
        )
    sub = lax.broadcasted_iota(jnp.int32, (8, LANE), 0)
    tap = lax.broadcasted_iota(jnp.int32, (8, LANE), 1) // COMP
    pick_re = sub == tap
    pick_im = sub - TAPS == tap
    blank = jnp.zeros((64, LANE), jnp.bfloat16)

    def step(g):
        cols = jnp.concatenate(
            [c[n, g].astype(jnp.float32) for c in col_refs for n in range(2)], 0
        ).astype(jnp.bfloat16)
        rhs = jnp.concatenate(
            [jnp.concatenate([cols, blank], 1), jnp.concatenate([blank, cols], 1)], 0
        )
        pairs = []
        for pair in range(16):
            halves = []
            for half in range(2):
                i = 2 * pair + half
                at = (i // 8) * 1024 + g * 8 + i % 8
                re = rows[pl.ds(at, 8, stride=0), :]
                im = rows[pl.ds(4096 + at, 8, stride=0), :]
                halves.append(jnp.where(pick_re, re, jnp.where(pick_im, im, 0.0)))
            pairs.append(jnp.concatenate(halves, 1))
        lhs = jnp.concatenate(pairs, 0).astype(jnp.bfloat16)
        prod = lax.dot_general(
            lhs, rhs, (((1,), (1,)), ((), ())), preferred_element_type=jnp.float32
        )
        at = pl.multiple_of(g * 8, 8)
        for pair in range(16):
            cross[pair, pl.ds(at, 8), :] = prod[pair * 8 : pair * 8 + 8]

    def steps(k, carry):
        for u in range(UNROLL):
            step(k * UNROLL + u)
        return carry

    lax.fori_loop(0, LANE // UNROLL, steps, 0)
    table = table_ref[...]
    for d in range(4):
        for quad in range(2):
            pair = d * 4 + quad * 2
            weights = jnp.concatenate([cross[pair], cross[pair + 1]], 1).astype(jnp.bfloat16)
            lags = jnp.dot(table, weights, preferred_element_type=jnp.float32)
            out_refs[d][quad] = (lags * factor).astype(jnp.bfloat16)


def correlate(row_blocks, col_blocks, table, factor):
    def body(*refs):
        corr_kernel(factor, *refs)

    return pl.pallas_call(
        body,
        out_shape=[jax.ShapeDtypeStruct((2, LAG_ROWS, 256), jnp.bfloat16)] * 4,
        scratch_shapes=[
            pltpu.VMEM((8 * 1024, LANE), jnp.float32),
            pltpu.VMEM((16, 1024, LANE), jnp.float32),
        ],
        compiler_params=vmem(24),
        cost_estimate=pl.CostEstimate(
            flops=2 * LANE * LANE * 256 * LANE + 16 * LAG_ROWS * 1024 * 256,
            transcendentals=0,
            bytes_accessed=7 * 1024 * 1024,
        ),
        name="correlate",
    )(*row_blocks, *col_blocks, table)


def finish_kernel(member_ref, *refs):
    parts, order_ref, out_ref, buf = refs[:8], refs[8], refs[9], refs[10]
    z = member_ref[0] // 16
    pair = pl.program_id(0)
    at = pl.multiple_of(pair % 2 * LANE, LANE)
    for half in range(2):
        for far in range(2):
            wide = jnp.concatenate(
                [p[pair // 2, :, pl.ds(at, LANE)] for p in parts[far * 4 : far * 4 + 4]], 1
            )
            ordered = jnp.dot(wide, order_ref[far, half], preferred_element_type=jnp.float32)
            tile = z ^ far
            for r in range(2):
                buf[pl.ds(half * 4 * LAGS + tile * 2 + r, LAGS, stride=4), :] = ordered[
                    :LAGS, r * LANE : (r + 1) * LANE
                ]
    out_ref[0] = buf[...].astype(jnp.bfloat16)


def finish(member, parts, order):
    whole = pl.BlockSpec(memory_space=pltpu.VMEM)
    return pl.pallas_call(
        finish_kernel,
        grid=(4,),
        in_specs=[pl.BlockSpec(memory_space=pltpu.SMEM)] + [whole] * 9,
        out_specs=pl.BlockSpec((1, 8 * LAGS, LANE), lambda i: (i, 0, 0)),
        out_shape=jax.ShapeDtypeStruct((4, 8 * LAGS, LANE), jnp.bfloat16),
        scratch_shapes=[pltpu.VMEM((8 * LAGS, LANE), jnp.float32)],
        compiler_params=vmem(18),
        name="finish",
    )(member, *parts, order)


def lag_table(zero):
    lag = jnp.arange(LAG_ROWS, dtype=jnp.int32)[:, None] + zero
    k = jnp.arange(2 * BINS, dtype=jnp.int32)[None, :]
    frequency = k % TAPS * LANE + k // 8
    n = frequency * (lag - BINS // 2) + k // TAPS % 2 * (BINS // 2)
    turn = (n + BINS // 4) // (BINS // 2)
    x = (n - turn * (BINS // 2)).astype(jnp.float32) * (math.pi / BINS)
    x2 = x * x
    cos, sin = jnp.float32(0), jnp.float32(0)
    for power in range(10, -1, -2):
        cos = cos * x2 + (-1) ** (power // 2) / math.factorial(power)
        sin = sin * x2 + (-1) ** (power // 2) / math.factorial(power + 1)
    values = jnp.where(turn % 2 == 0, cos, sin * x)
    values = jnp.where((turn + 1) // 2 % 2 == 0, values, -values)
    return jnp.where(lag < LAGS, values, 0.0).astype(jnp.bfloat16)


def column_order(member):
    x, y = member // 4 % 4, member % 4
    at = jnp.arange(512, dtype=jnp.int32)
    d, half, e, turn, ch = at // 128, at // 64 % 2, at // 16 % 4, at // 8 % 2, at % 8
    first = (x ^ d) * 32 + (y ^ e) * 8 + ch
    second = (x ^ e) * 32 + (y ^ d) * 8 + ch
    target = jnp.stack([first, second], 0) + (128 * turn + 256 * half)[None]
    column = jnp.arange(256, dtype=jnp.int32)[None, None, None, :]
    side = jnp.arange(2, dtype=jnp.int32)[None, :, None, None]
    return (target[:, None, :, None] == column + 256 * side).astype(jnp.bfloat16)


def on_device(spectra, partners):
    member = lax.axis_index("mem").astype(jnp.int32)
    where = jnp.stack([member, lax.axis_index("grp").astype(jnp.int32) >> 1])
    factor = math.sqrt(2.0 / (BINS * (COMP // 2)))
    white = whiten(spectra)

    row_masks, col_masks = (4, 1), (1, 4)
    rows = [[white, None, None, None], [white, None, None, None]]

    for d in (1, 3):
        rows[1][d] = xor_perm(white, "mem", d * row_masks[1])
    up, down = ring_perm(white, 1), ring_perm(white, -1)
    up, down, rows, source = lax.optimization_barrier((up, down, rows, white))
    for n in range(2):
        rows[n][2] = xor_perm(source, "mem", 2 * row_masks[n])
    tops = [ring_perm(up[: LANE // 2], 1), ring_perm(down[LANE // 2 :], -1)]
    up, down, tops, rows, where = lax.optimization_barrier((up, down, tops, rows, where))

    mine = choose(pick_kernel, "pick", where, partners, [white, down, up, *tops])
    other = xor_perm(mine, "grp", 1)
    near = choose(merge_kernel, "merge", where, partners, [mine, other])
    near, where, source = lax.optimization_barrier((near, where, white))
    for d in (3, 1):
        rows[0][d] = xor_perm(source, "mem", d * row_masks[0])
    across = xor_perm(near, "mem", 16)
    cols = [[near, None, None, None], [across, None, None, None]]
    for e in (3, 1):
        cols[0][e] = xor_perm(near, "mem", e * col_masks[0])
    table = lag_table(where[0] - member)
    order = column_order(where[0])
    cols, rows, near, across, table, order = lax.optimization_barrier(
        (cols, rows, near, across, table, order)
    )
    for e in (3, 1):
        cols[1][e] = xor_perm(across, "mem", e * col_masks[1])
    cols[0][2] = xor_perm(near, "mem", 2 * col_masks[0])
    cols, across = lax.optimization_barrier((cols, across))
    cols[1][2] = xor_perm(across, "mem", 2 * col_masks[1])
    parts = []
    for n in range(2):
        sums = correlate(rows[n], cols[n], table, factor)
        parts += [sums[0]] + [xor_perm(sums[d], "mem", d * row_masks[n]) for d in range(1, 4)]
        cols[1], sums = lax.optimization_barrier((cols[1], sums[0]))
    packed = finish(member.reshape(1), parts, order)
    result = packed.reshape(CH, LAGS, 2, 2, LANE)
    return jnp.transpose(result, (0, 3, 2, 4, 1)).reshape(CH, 2, 256, LAGS)


def solution(mesh):
    placed = (P(("grp", "mem"), None, None, None), P())
    return jax.shard_map(
        on_device,
        mesh=mesh,
        in_specs=placed,
        out_specs=P(("grp", "mem"), None, None, None),
        check_vma=False,
    )
```

```python
import math

import jax
import jax.numpy as jnp
from jax import lax
from jax.experimental import pallas as pl
from jax.experimental.pallas import tpu as pltpu
from jax.sharding import PartitionSpec as P

SMOOTH = 32
CH = 8
COMP = 32
BINS = 512
LANE = 128
TAPS = BINS // LANE
LAGS = BINS + 1
LAG_ROWS = 520
UNROLL = 16


def vmem(mib):
    return pltpu.CompilerParams(vmem_limit_bytes=mib * 1024 * 1024)


def xor_perm(array, axis, mask):
    return lax.ppermute(array, axis, [(i, i ^ mask) for i in range(lax.axis_size(axis))])


def ring_perm(array, shift):
    size = lax.axis_size("grp")
    return lax.ppermute(array, "grp", [(i, (i + 2 * shift) % size) for i in range(size)])


def whiten_kernel(spectra_ref, out_ref, rows):
    comps = spectra_ref[...].astype(jnp.float32)
    power = (comps[:, 0] * comps[:, 0] + comps[:, 1] * comps[:, 1]).reshape(-1, BINS)
    row = lax.broadcasted_iota(jnp.int32, (BINS, BINS), 0)
    col = lax.broadcasted_iota(jnp.int32, (BINS, BINS), 1)
    band = (jnp.abs(row - col) <= SMOOTH).astype(jnp.float32)
    smooth = jnp.dot(
        power, band, precision=lax.Precision.HIGHEST, preferred_element_type=jnp.float32
    )
    inv = lax.rsqrt(smooth / (2 * SMOOTH + 1) + 1e-05)
    segs = COMP // 2
    for ch in range(CH):
        level = inv[ch * segs : (ch + 1) * segs]
        white = jnp.concatenate([comps[ch, 0] * level, comps[ch, 1] * level], 0)
        taps = jnp.concatenate([white[:, k * LANE : (k + 1) * LANE] for k in range(TAPS)], 0)
        rows[pl.ds(ch, LANE, stride=CH), :] = taps.T
    out_ref[...] = rows[...].reshape(LANE, CH, LANE).astype(jnp.bfloat16)


def whiten(spectra):
    return pl.pallas_call(
        whiten_kernel,
        out_shape=jax.ShapeDtypeStruct((LANE, CH, LANE), jnp.bfloat16),
        scratch_shapes=[pltpu.VMEM((LANE * CH, LANE), jnp.float32)],
        compiler_params=vmem(10),
        name="whiten",
    )(spectra)


def pick_kernel(where_ref, partners_ref, *refs):
    blocks, tops, out_ref = refs[:3], refs[3:5], refs[5]
    here = where_ref[1]
    for r in range(2):
        shift = ((here ^ (partners_ref[r, where_ref[0]] >> 1)) - here) & 3
        for s in range(4):

            @pl.when(shift == s)
            def _():
                if s == 2:
                    out_ref[r, : LANE // 2] = tops[0][...]
                    out_ref[r, LANE // 2 :] = tops[1][...]
                else:
                    out_ref[r] = blocks[s - (s > 2)][...]


def merge_kernel(where_ref, partners_ref, mine_ref, other_ref, out_ref):
    for r in range(2):
        swap = partners_ref[r, where_ref[0]] & 1

        @pl.when(swap == 1)
        def _():
            out_ref[r] = other_ref[r]

        @pl.when(swap == 0)
        def _():
            out_ref[r] = mine_ref[r]


def choose(kernel, name, where, partners, arrays):
    smem, whole = pl.BlockSpec(memory_space=pltpu.SMEM), pl.BlockSpec(memory_space=pltpu.VMEM)
    return pl.pallas_call(
        kernel,
        in_specs=[smem, smem] + [whole] * len(arrays),
        out_shape=jax.ShapeDtypeStruct((2, LANE, CH, LANE), jnp.bfloat16),
        compiler_params=vmem(10),
        name=name,
    )(where, partners, *arrays)


def corr_kernel(factor, *refs):
    row_refs, col_refs, table_ref = refs[:4], refs[4:8], refs[8]
    out_refs, rows, cross = refs[9:13], refs[13], refs[14]
    lane = lax.broadcasted_iota(jnp.int32, (CH * LANE, LANE), 1)
    imag = lane // 16 % 2 == 1
    for d in range(4):
        own = row_refs[d][...].astype(jnp.float32).reshape(CH * LANE, LANE)
        rows[pl.ds(d * 1024, 1024), :] = own
        rows[pl.ds(4096 + d * 1024, 1024), :] = jnp.where(
            imag, -pltpu.roll(own, 16, 1), pltpu.roll(own, LANE - 16, 1)
        )
    sub = lax.broadcasted_iota(jnp.int32, (8, LANE), 0)
    tap = lax.broadcasted_iota(jnp.int32, (8, LANE), 1) // COMP
    pick_re = sub == tap
    pick_im = sub - TAPS == tap
    blank = jnp.zeros((64, LANE), jnp.bfloat16)

    def step(g):
        cols = jnp.concatenate(
            [c[n, g].astype(jnp.float32) for c in col_refs for n in range(2)], 0
        ).astype(jnp.bfloat16)
        rhs = jnp.concatenate(
            [jnp.concatenate([cols, blank], 1), jnp.concatenate([blank, cols], 1)], 0
        )
        pairs = []
        for pair in range(16):
            halves = []
            for half in range(2):
                i = 2 * pair + half
                at = (i // 8) * 1024 + g * 8 + i % 8
                re = rows[pl.ds(at, 8, stride=0), :]
                im = rows[pl.ds(4096 + at, 8, stride=0), :]
                halves.append(jnp.where(pick_re, re, jnp.where(pick_im, im, 0.0)))
            pairs.append(jnp.concatenate(halves, 1))
        lhs = jnp.concatenate(pairs, 0).astype(jnp.bfloat16)
        prod = lax.dot_general(
            lhs, rhs, (((1,), (1,)), ((), ())), preferred_element_type=jnp.float32
        )
        at = pl.multiple_of(g * 8, 8)
        for pair in range(16):
            cross[pair, pl.ds(at, 8), :] = prod[pair * 8 : pair * 8 + 8]

    def steps(k, carry):
        for u in range(UNROLL):
            step(k * UNROLL + u)
        return carry

    lax.fori_loop(0, LANE // UNROLL, steps, 0)
    table = table_ref[...]
    for d in range(4):
        for quad in range(2):
            pair = d * 4 + quad * 2
            weights = jnp.concatenate([cross[pair], cross[pair + 1]], 1).astype(jnp.bfloat16)
            lags = jnp.dot(table, weights, preferred_element_type=jnp.float32)
            out_refs[d][quad] = (lags * factor).astype(jnp.bfloat16)


def correlate(row_blocks, col_blocks, table, factor):
    def body(*refs):
        corr_kernel(factor, *refs)

    return pl.pallas_call(
        body,
        out_shape=[jax.ShapeDtypeStruct((2, LAG_ROWS, 256), jnp.bfloat16)] * 4,
        scratch_shapes=[
            pltpu.VMEM((8 * 1024, LANE), jnp.float32),
            pltpu.VMEM((16, 1024, LANE), jnp.float32),
        ],
        compiler_params=vmem(24),
        cost_estimate=pl.CostEstimate(
            flops=2 * LANE * LANE * 256 * LANE + 16 * LAG_ROWS * 1024 * 256,
            transcendentals=0,
            bytes_accessed=7 * 1024 * 1024,
        ),
        name="correlate",
    )(*row_blocks, *col_blocks, table)


def finish_kernel(member_ref, *refs):
    parts, order_ref, out_ref, buf = refs[:8], refs[8], refs[9], refs[10]
    z = member_ref[0] // 16
    pair = pl.program_id(0)
    at = pl.multiple_of(pair % 2 * LANE, LANE)
    for half in range(2):
        for far in range(2):
            wide = jnp.concatenate(
                [p[pair // 2, :, pl.ds(at, LANE)] for p in parts[far * 4 : far * 4 + 4]], 1
            )
            ordered = jnp.dot(wide, order_ref[far, half], preferred_element_type=jnp.float32)
            tile = z ^ far
            for r in range(2):
                buf[pl.ds(half * 4 * LAGS + tile * 2 + r, LAGS, stride=4), :] = ordered[
                    :LAGS, r * LANE : (r + 1) * LANE
                ]
    out_ref[0] = buf[...].astype(jnp.bfloat16)


def finish(member, parts, order):
    whole = pl.BlockSpec(memory_space=pltpu.VMEM)
    return pl.pallas_call(
        finish_kernel,
        grid=(4,),
        in_specs=[pl.BlockSpec(memory_space=pltpu.SMEM)] + [whole] * 9,
        out_specs=pl.BlockSpec((1, 8 * LAGS, LANE), lambda i: (i, 0, 0)),
        out_shape=jax.ShapeDtypeStruct((4, 8 * LAGS, LANE), jnp.bfloat16),
        scratch_shapes=[pltpu.VMEM((8 * LAGS, LANE), jnp.float32)],
        compiler_params=vmem(18),
        name="finish",
    )(member, *parts, order)


def lag_table(zero):
    lag = jnp.arange(LAG_ROWS, dtype=jnp.int32)[:, None] + zero
    k = jnp.arange(2 * BINS, dtype=jnp.int32)[None, :]
    frequency = k % TAPS * LANE + k // 8
    n = frequency * (lag - BINS // 2) + k // TAPS % 2 * (BINS // 2)
    turn = (n + BINS // 4) // (BINS // 2)
    x = (n - turn * (BINS // 2)).astype(jnp.float32) * (math.pi / BINS)
    x2 = x * x
    cos, sin = jnp.float32(0), jnp.float32(0)
    for power in range(10, -1, -2):
        cos = cos * x2 + (-1) ** (power // 2) / math.factorial(power)
        sin = sin * x2 + (-1) ** (power // 2) / math.factorial(power + 1)
    values = jnp.where(turn % 2 == 0, cos, sin * x)
    values = jnp.where((turn + 1) // 2 % 2 == 0, values, -values)
    return jnp.where(lag < LAGS, values, 0.0).astype(jnp.bfloat16)


def column_order(member):
    x, y = member // 4 % 4, member % 4
    at = jnp.arange(512, dtype=jnp.int32)
    d, half, e, turn, ch = at // 128, at // 64 % 2, at // 16 % 4, at // 8 % 2, at % 8
    first = (x ^ d) * 32 + (y ^ e) * 8 + ch
    second = (x ^ e) * 32 + (y ^ d) * 8 + ch
    target = jnp.stack([first, second], 0) + (128 * turn + 256 * half)[None]
    column = jnp.arange(256, dtype=jnp.int32)[None, None, None, :]
    side = jnp.arange(2, dtype=jnp.int32)[None, :, None, None]
    return (target[:, None, :, None] == column + 256 * side).astype(jnp.bfloat16)


def on_device(spectra, partners):
    member = lax.axis_index("mem").astype(jnp.int32)
    where = jnp.stack([member, lax.axis_index("grp").astype(jnp.int32) >> 1])
    factor = math.sqrt(2.0 / (BINS * (COMP // 2)))
    white = whiten(spectra)

    row_masks, col_masks = (4, 1), (1, 4)
    rows = [[white, None, None, None], [white, None, None, None]]

    for d in (1, 2, 3):
        rows[0][d] = xor_perm(white, "mem", d * row_masks[0])
    up, down = ring_perm(white, 1), ring_perm(white, -1)
    source, rows[0] = lax.optimization_barrier((white, rows[0]))
    for d in (1, 3):
        rows[1][d] = xor_perm(source, "mem", d * row_masks[1])
    rows, source, up, down = lax.optimization_barrier((rows, source, up, down))
    source, *halves = lax.optimization_barrier((source, up[: LANE // 2], down[LANE // 2 :]))
    rows[1][2] = xor_perm(source, "mem", 2 * row_masks[1])
    tops = [ring_perm(halves[0], 1), ring_perm(halves[1], -1)]
    rows, where, up, down, tops = lax.optimization_barrier((rows, where, up, down, tops))

    mine = choose(pick_kernel, "pick", where, partners, [white, down, up, *tops])
    other = xor_perm(mine, "grp", 1)
    near = choose(merge_kernel, "merge", where, partners, [mine, other])
    near, where = lax.optimization_barrier((near, where))
    across = xor_perm(near, "mem", 16)
    hop = xor_perm(near, "mem", 2 * col_masks[1])
    near1, near3 = [xor_perm(near, "mem", e * col_masks[0]) for e in (1, 3)]
    table = lag_table(where[0] - member)
    order = column_order(where[0])
    table, order, near, near1, near3, hop, across = lax.optimization_barrier(
        (table, order, near, near1, near3, hop, across)
    )
    near2 = xor_perm(near, "mem", 2 * col_masks[0])
    far2 = xor_perm(hop, "mem", 16)
    far3 = xor_perm(across, "mem", 3 * col_masks[1])
    across, near2, far3, far2 = lax.optimization_barrier((across, near2, far3, far2))
    far1 = xor_perm(across, "mem", col_masks[1])
    cols = [[near, near1, near2, near3], [across, far1, far2, far3]]
    parts = []
    for n in range(2):
        sums = correlate(rows[n], cols[n], table, factor)
        parts += [sums[0]] + [xor_perm(sums[d], "mem", d * row_masks[n]) for d in range(1, 4)]
        cols[1], sums = lax.optimization_barrier((cols[1], sums[0]))
    packed = finish(member.reshape(1), parts, order)
    result = packed.reshape(CH, LAGS, 2, 2, LANE)
    return jnp.transpose(result, (0, 3, 2, 4, 1)).reshape(CH, 2, 256, LAGS)


def solution(mesh):
    placed = (P(("grp", "mem"), None, None, None), P())
    return jax.shard_map(
        on_device,
        mesh=mesh,
        in_specs=placed,
        out_specs=P(("grp", "mem"), None, None, None),
        check_vma=False,
    )
```

```python
import math

import jax
import jax.numpy as jnp
from jax import lax
from jax.experimental import pallas as pl
from jax.experimental.pallas import tpu as pltpu
from jax.sharding import PartitionSpec as P

SMOOTH = 32
CH = 8
COMP = 32
BINS = 512
LANE = 128
TAPS = BINS // LANE
LAGS = BINS + 1
LAG_ROWS = 520
UNROLL = 16


def vmem(mib):
    return pltpu.CompilerParams(vmem_limit_bytes=mib * 1024 * 1024)


def xor_perm(array, axis, mask):
    return lax.ppermute(array, axis, [(i, i ^ mask) for i in range(lax.axis_size(axis))])


def ring_perm(array, shift):
    size = lax.axis_size("grp")
    return lax.ppermute(array, "grp", [(i, (i + 2 * shift) % size) for i in range(size)])


def whiten_kernel(spectra_ref, out_ref, rows):
    comps = spectra_ref[...].astype(jnp.float32)
    power = (comps[:, 0] * comps[:, 0] + comps[:, 1] * comps[:, 1]).reshape(-1, BINS)
    row = lax.broadcasted_iota(jnp.int32, (BINS, BINS), 0)
    col = lax.broadcasted_iota(jnp.int32, (BINS, BINS), 1)
    band = (jnp.abs(row - col) <= SMOOTH).astype(jnp.float32)
    smooth = jnp.dot(
        power, band, precision=lax.Precision.HIGHEST, preferred_element_type=jnp.float32
    )
    inv = lax.rsqrt(smooth / (2 * SMOOTH + 1) + 1e-05)
    segs = COMP // 2
    for ch in range(CH):
        level = inv[ch * segs : (ch + 1) * segs]
        white = jnp.concatenate([comps[ch, 0] * level, comps[ch, 1] * level], 0)
        taps = jnp.concatenate([white[:, k * LANE : (k + 1) * LANE] for k in range(TAPS)], 0)
        rows[pl.ds(ch, LANE, stride=CH), :] = taps.T
    out_ref[...] = rows[...].reshape(LANE, CH, LANE).astype(jnp.bfloat16)


def whiten(spectra):
    return pl.pallas_call(
        whiten_kernel,
        out_shape=jax.ShapeDtypeStruct((LANE, CH, LANE), jnp.bfloat16),
        scratch_shapes=[pltpu.VMEM((LANE * CH, LANE), jnp.float32)],
        compiler_params=vmem(10),
        name="whiten",
    )(spectra)


def pick_kernel(where_ref, partners_ref, *refs):
    blocks, tops, out_ref = refs[:3], refs[3:5], refs[5]
    here = where_ref[1]
    for r in range(2):
        shift = ((here ^ (partners_ref[r, where_ref[0]] >> 1)) - here) & 3
        for s in range(4):

            @pl.when(shift == s)
            def _():
                if s == 2:
                    out_ref[r, : LANE // 2] = tops[0][...]
                    out_ref[r, LANE // 2 :] = tops[1][...]
                else:
                    out_ref[r] = blocks[s - (s > 2)][...]


def merge_kernel(where_ref, partners_ref, mine_ref, other_ref, out_ref):
    for r in range(2):
        swap = partners_ref[r, where_ref[0]] & 1

        @pl.when(swap == 1)
        def _():
            out_ref[r] = other_ref[r]

        @pl.when(swap == 0)
        def _():
            out_ref[r] = mine_ref[r]


def choose(kernel, name, where, partners, arrays):
    smem, whole = pl.BlockSpec(memory_space=pltpu.SMEM), pl.BlockSpec(memory_space=pltpu.VMEM)
    return pl.pallas_call(
        kernel,
        in_specs=[smem, smem] + [whole] * len(arrays),
        out_shape=jax.ShapeDtypeStruct((2, LANE, CH, LANE), jnp.bfloat16),
        compiler_params=vmem(10),
        name=name,
    )(where, partners, *arrays)


def corr_kernel(factor, *refs):
    row_refs, col_refs, table_ref = refs[:4], refs[4:8], refs[8]
    out_refs, rows, cross = refs[9:13], refs[13], refs[14]
    lane = lax.broadcasted_iota(jnp.int32, (CH * LANE, LANE), 1)
    imag = lane // 16 % 2 == 1
    for d in range(4):
        own = row_refs[d][...].astype(jnp.float32).reshape(CH * LANE, LANE)
        rows[pl.ds(d * 1024, 1024), :] = own
        rows[pl.ds(4096 + d * 1024, 1024), :] = jnp.where(
            imag, -pltpu.roll(own, 16, 1), pltpu.roll(own, LANE - 16, 1)
        )
    sub = lax.broadcasted_iota(jnp.int32, (8, LANE), 0)
    tap = lax.broadcasted_iota(jnp.int32, (8, LANE), 1) // COMP
    pick_re = sub == tap
    pick_im = sub - TAPS == tap
    blank = jnp.zeros((64, LANE), jnp.bfloat16)

    def step(g):
        cols = jnp.concatenate(
            [c[n, g].astype(jnp.float32) for c in col_refs for n in range(2)], 0
        ).astype(jnp.bfloat16)
        rhs = jnp.concatenate(
            [jnp.concatenate([cols, blank], 1), jnp.concatenate([blank, cols], 1)], 0
        )
        pairs = []
        for pair in range(16):
            halves = []
            for half in range(2):
                i = 2 * pair + half
                at = (i // 8) * 1024 + g * 8 + i % 8
                re = rows[pl.ds(at, 8, stride=0), :]
                im = rows[pl.ds(4096 + at, 8, stride=0), :]
                halves.append(jnp.where(pick_re, re, jnp.where(pick_im, im, 0.0)))
            pairs.append(jnp.concatenate(halves, 1))
        lhs = jnp.concatenate(pairs, 0).astype(jnp.bfloat16)
        prod = lax.dot_general(
            lhs, rhs, (((1,), (1,)), ((), ())), preferred_element_type=jnp.float32
        )
        at = pl.multiple_of(g * 8, 8)
        for pair in range(16):
            cross[pair, pl.ds(at, 8), :] = prod[pair * 8 : pair * 8 + 8]

    def steps(k, carry):
        for u in range(UNROLL):
            step(k * UNROLL + u)
        return carry

    lax.fori_loop(0, LANE // UNROLL, steps, 0)
    table = table_ref[...]
    for d in range(4):
        for quad in range(2):
            pair = d * 4 + quad * 2
            weights = jnp.concatenate([cross[pair], cross[pair + 1]], 1).astype(jnp.bfloat16)
            lags = jnp.dot(table, weights, preferred_element_type=jnp.float32)
            out_refs[d][quad] = (lags * factor).astype(jnp.bfloat16)


def correlate(row_blocks, col_blocks, table, factor):
    def body(*refs):
        corr_kernel(factor, *refs)

    return pl.pallas_call(
        body,
        out_shape=[jax.ShapeDtypeStruct((2, LAG_ROWS, 256), jnp.bfloat16)] * 4,
        scratch_shapes=[
            pltpu.VMEM((8 * 1024, LANE), jnp.float32),
            pltpu.VMEM((16, 1024, LANE), jnp.float32),
        ],
        compiler_params=vmem(24),
        cost_estimate=pl.CostEstimate(
            flops=2 * LANE * LANE * 256 * LANE + 16 * LAG_ROWS * 1024 * 256,
            transcendentals=0,
            bytes_accessed=7 * 1024 * 1024,
        ),
        name="correlate",
    )(*row_blocks, *col_blocks, table)


def finish_kernel(member_ref, *refs):
    parts, order_ref, out_ref, buf = refs[:8], refs[8], refs[9], refs[10]
    z = member_ref[0] // 16
    pair = pl.program_id(0)
    at = pl.multiple_of(pair % 2 * LANE, LANE)
    for half in range(2):
        for far in range(2):
            wide = jnp.concatenate(
                [p[pair // 2, :, pl.ds(at, LANE)] for p in parts[far * 4 : far * 4 + 4]], 1
            )
            ordered = jnp.dot(wide, order_ref[far, half], preferred_element_type=jnp.float32)
            tile = z ^ far
            for r in range(2):
                buf[pl.ds(half * 4 * LAGS + tile * 2 + r, LAGS, stride=4), :] = ordered[
                    :LAGS, r * LANE : (r + 1) * LANE
                ]
    out_ref[0] = buf[...].astype(jnp.bfloat16)


def finish(member, parts, order):
    whole = pl.BlockSpec(memory_space=pltpu.VMEM)
    return pl.pallas_call(
        finish_kernel,
        grid=(4,),
        in_specs=[pl.BlockSpec(memory_space=pltpu.SMEM)] + [whole] * 9,
        out_specs=pl.BlockSpec((1, 8 * LAGS, LANE), lambda i: (i, 0, 0)),
        out_shape=jax.ShapeDtypeStruct((4, 8 * LAGS, LANE), jnp.bfloat16),
        scratch_shapes=[pltpu.VMEM((8 * LAGS, LANE), jnp.float32)],
        compiler_params=vmem(18),
        name="finish",
    )(member, *parts, order)


def lag_table(zero):
    lag = jnp.arange(LAG_ROWS, dtype=jnp.int32)[:, None] + zero
    k = jnp.arange(2 * BINS, dtype=jnp.int32)[None, :]
    frequency = k % TAPS * LANE + k // 8
    n = frequency * (lag - BINS // 2) + k // TAPS % 2 * (BINS // 2)
    turn = (n + BINS // 4) >> 8
    x = (n - (turn << 8)).astype(jnp.float32) * (math.pi / BINS)
    x2 = x * x
    cos, sin = jnp.float32(0), jnp.float32(0)
    for power in range(10, -1, -2):
        cos = cos * x2 + (-1) ** (power // 2) / math.factorial(power)
        sin = sin * x2 + (-1) ** (power // 2) / math.factorial(power + 1)
    values = jnp.where(turn & 1 == 0, cos, sin * x)
    values = jnp.where((turn + 1) & 2 == 0, values, -values)
    return jnp.where(lag < LAGS, values, 0.0).astype(jnp.bfloat16)


def column_order(member):
    x, y = member // 4 % 4, member % 4
    at = jnp.arange(512, dtype=jnp.int32)
    d, half, e, turn, ch = at // 128, at // 64 % 2, at // 16 % 4, at // 8 % 2, at % 8
    first = (x ^ d) * 32 + (y ^ e) * 8 + ch
    second = (x ^ e) * 32 + (y ^ d) * 8 + ch
    target = jnp.stack([first, second], 0) + (128 * turn + 256 * half)[None]
    column = jnp.arange(256, dtype=jnp.int32)[None, None, None, :]
    side = jnp.arange(2, dtype=jnp.int32)[None, :, None, None]
    return (target[:, None, :, None] == column + 256 * side).astype(jnp.bfloat16)


def on_device(spectra, partners):
    member = lax.axis_index("mem").astype(jnp.int32)
    plane = lax.axis_index("grp").astype(jnp.int32) >> 1
    factor = math.sqrt(2.0 / (BINS * (COMP // 2)))
    white = whiten(spectra)

    row_masks, col_masks = (4, 1), (1, 4)
    rows = [[white, None, None, None], [white, None, None, None]]

    for d in (1, 2, 3):
        rows[0][d] = xor_perm(white, "mem", d * row_masks[0])
    up, down = ring_perm(white, 1), ring_perm(white, -1)
    rows, source, up, down = lax.optimization_barrier((rows, white, up, down))
    member_now, *halves = lax.optimization_barrier((member, up[: LANE // 2], down[LANE // 2 :]))
    where = jnp.stack([member_now, plane])
    source, where = lax.optimization_barrier((source, where))
    for d in (1, 2, 3):
        rows[1][d] = xor_perm(source, "mem", d * row_masks[1])
    tops = [ring_perm(halves[0], 1), ring_perm(halves[1], -1)]
    rows, where, up, down, tops = lax.optimization_barrier((rows, where, up, down, tops))

    mine = choose(pick_kernel, "pick", where, partners, [white, down, up, *tops])
    other = xor_perm(mine, "grp", 1)
    near = choose(merge_kernel, "merge", where, partners, [mine, other])
    near, where = lax.optimization_barrier((near, where))
    across = xor_perm(near, "mem", 16)
    hop = xor_perm(near, "mem", 2 * col_masks[1])
    order = column_order(where[0])
    later, order = lax.optimization_barrier((near, order))
    near1, near2, near3 = [xor_perm(later, "mem", e * col_masks[0]) for e in (1, 2, 3)]
    table = lag_table(where[0] - member)
    table, order, hop, across = lax.optimization_barrier((table, order, hop, across))
    far2 = xor_perm(hop, "mem", 16)
    far3 = xor_perm(across, "mem", 3 * col_masks[1])
    across, near1, near2, near3, far2, far3 = lax.optimization_barrier(
        (across, near1, near2, near3, far2, far3)
    )
    far1 = xor_perm(across, "mem", col_masks[1])
    cols = [[near, near1, near2, near3], [across, far1, far2, far3]]
    parts = []
    for n in range(2):
        sums = correlate(rows[n], cols[n], table, factor)
        parts += [sums[0]] + [xor_perm(sums[d], "mem", d * row_masks[n]) for d in range(1, 4)]
        cols[1], sums = lax.optimization_barrier((cols[1], sums[0]))
    packed = finish(member.reshape(1), parts, order)
    result = packed.reshape(CH, LAGS, 2, 2, LANE)
    return jnp.transpose(result, (0, 3, 2, 4, 1)).reshape(CH, 2, 256, LAGS)


def solution(mesh):
    placed = (P(("grp", "mem"), None, None, None), P())
    return jax.shard_map(
        on_device,
        mesh=mesh,
        in_specs=placed,
        out_specs=P(("grp", "mem"), None, None, None),
        check_vma=False,
    )
```

```python
import math

import jax
import jax.numpy as jnp
from jax import lax
from jax.experimental import pallas as pl
from jax.experimental.pallas import tpu as pltpu
from jax.sharding import PartitionSpec as P

SMOOTH = 32
CH = 8
COMP = 32
BINS = 512
LANE = 128
TAPS = BINS // LANE
LAGS = BINS + 1
LAG_ROWS = 520
UNROLL = 16


def vmem(mib):
    return pltpu.CompilerParams(vmem_limit_bytes=mib * 1024 * 1024)


def xor_perm(array, axis, mask):
    return lax.ppermute(array, axis, [(i, i ^ mask) for i in range(lax.axis_size(axis))])


def ring_perm(array, shift):
    size = lax.axis_size("grp")
    return lax.ppermute(array, "grp", [(i, (i + 2 * shift) % size) for i in range(size)])


def whiten_kernel(spectra_ref, out_ref, rows):
    comps = spectra_ref[...].astype(jnp.float32)
    power = (comps[:, 0] * comps[:, 0] + comps[:, 1] * comps[:, 1]).reshape(-1, BINS)
    row = lax.broadcasted_iota(jnp.int32, (BINS, BINS), 0)
    col = lax.broadcasted_iota(jnp.int32, (BINS, BINS), 1)
    band = (jnp.abs(row - col) <= SMOOTH).astype(jnp.float32)
    smooth = jnp.dot(
        power, band, precision=lax.Precision.HIGHEST, preferred_element_type=jnp.float32
    )
    inv = lax.rsqrt(smooth / (2 * SMOOTH + 1) + 1e-05)
    segs = COMP // 2
    for ch in range(CH):
        level = inv[ch * segs : (ch + 1) * segs]
        white = jnp.concatenate([comps[ch, 0] * level, comps[ch, 1] * level], 0)
        taps = jnp.concatenate([white[:, k * LANE : (k + 1) * LANE] for k in range(TAPS)], 0)
        rows[pl.ds(ch, LANE, stride=CH), :] = taps.T
    out_ref[...] = rows[...].reshape(LANE, CH, LANE).astype(jnp.bfloat16)


def whiten(spectra):
    return pl.pallas_call(
        whiten_kernel,
        out_shape=jax.ShapeDtypeStruct((LANE, CH, LANE), jnp.bfloat16),
        scratch_shapes=[pltpu.VMEM((LANE * CH, LANE), jnp.float32)],
        compiler_params=vmem(10),
        name="whiten",
    )(spectra)


def pick_kernel(where_ref, partners_ref, *refs):
    blocks, tops, out_ref = refs[:3], refs[3:5], refs[5]
    here = where_ref[1]
    for r in range(2):
        shift = ((here ^ (partners_ref[r, where_ref[0]] >> 1)) - here) & 3
        for s in range(4):

            @pl.when(shift == s)
            def _():
                if s == 2:
                    out_ref[r, : LANE // 2] = tops[0][...]
                    out_ref[r, LANE // 2 :] = tops[1][...]
                else:
                    out_ref[r] = blocks[s - (s > 2)][...]


def merge_kernel(where_ref, partners_ref, mine_ref, other_ref, out_ref):
    for r in range(2):
        swap = partners_ref[r, where_ref[0]] & 1

        @pl.when(swap == 1)
        def _():
            out_ref[r] = other_ref[r]

        @pl.when(swap == 0)
        def _():
            out_ref[r] = mine_ref[r]


def choose(kernel, name, where, partners, arrays):
    smem, whole = pl.BlockSpec(memory_space=pltpu.SMEM), pl.BlockSpec(memory_space=pltpu.VMEM)
    return pl.pallas_call(
        kernel,
        in_specs=[smem, smem] + [whole] * len(arrays),
        out_shape=jax.ShapeDtypeStruct((2, LANE, CH, LANE), jnp.bfloat16),
        compiler_params=vmem(10),
        name=name,
    )(where, partners, *arrays)


def corr_kernel(factor, place_ref, row_ref, *refs):
    col_refs, table_ref = refs[:4], refs[4]
    out_refs, rows, cross = refs[5:9], refs[9], refs[10]
    lane = lax.broadcasted_iota(jnp.int32, (CH * LANE, LANE), 1)
    imag = lane // 16 % 2 == 1
    for d in range(4):
        own = row_ref[place_ref[0] ^ d].astype(jnp.float32).reshape(CH * LANE, LANE)
        rows[pl.ds(d * 1024, 1024), :] = own
        rows[pl.ds(4096 + d * 1024, 1024), :] = jnp.where(
            imag, -pltpu.roll(own, 16, 1), pltpu.roll(own, LANE - 16, 1)
        )
    sub = lax.broadcasted_iota(jnp.int32, (8, LANE), 0)
    tap = lax.broadcasted_iota(jnp.int32, (8, LANE), 1) // COMP
    pick_re = sub == tap
    pick_im = sub - TAPS == tap
    blank = jnp.zeros((64, LANE), jnp.bfloat16)

    def step(g):
        cols = jnp.concatenate(
            [c[n, g].astype(jnp.float32) for c in col_refs for n in range(2)], 0
        ).astype(jnp.bfloat16)
        rhs = jnp.concatenate(
            [jnp.concatenate([cols, blank], 1), jnp.concatenate([blank, cols], 1)], 0
        )
        pairs = []
        for pair in range(16):
            halves = []
            for half in range(2):
                i = 2 * pair + half
                at = (i // 8) * 1024 + g * 8 + i % 8
                re = rows[pl.ds(at, 8, stride=0), :]
                im = rows[pl.ds(4096 + at, 8, stride=0), :]
                halves.append(jnp.where(pick_re, re, jnp.where(pick_im, im, 0.0)))
            pairs.append(jnp.concatenate(halves, 1))
        lhs = jnp.concatenate(pairs, 0).astype(jnp.bfloat16)
        prod = lax.dot_general(
            lhs, rhs, (((1,), (1,)), ((), ())), preferred_element_type=jnp.float32
        )
        at = pl.multiple_of(g * 8, 8)
        for pair in range(16):
            cross[pair, pl.ds(at, 8), :] = prod[pair * 8 : pair * 8 + 8]

    def steps(k, carry):
        for u in range(UNROLL):
            step(k * UNROLL + u)
        return carry

    lax.fori_loop(0, LANE // UNROLL, steps, 0)
    table = table_ref[...]
    for d in range(4):
        for quad in range(2):
            pair = d * 4 + quad * 2
            weights = jnp.concatenate([cross[pair], cross[pair + 1]], 1).astype(jnp.bfloat16)
            lags = jnp.dot(table, weights, preferred_element_type=jnp.float32)
            out_refs[d][quad] = (lags * factor).astype(jnp.bfloat16)


def correlate(place, row_blocks, col_blocks, table, factor):
    def body(*refs):
        corr_kernel(factor, *refs)

    whole = pl.BlockSpec(memory_space=pltpu.VMEM)
    return pl.pallas_call(
        body,
        in_specs=[pl.BlockSpec(memory_space=pltpu.SMEM)] + [whole] * 6,
        out_shape=[jax.ShapeDtypeStruct((2, LAG_ROWS, 256), jnp.bfloat16)] * 4,
        scratch_shapes=[
            pltpu.VMEM((8 * 1024, LANE), jnp.float32),
            pltpu.VMEM((16, 1024, LANE), jnp.float32),
        ],
        compiler_params=vmem(20),
        cost_estimate=pl.CostEstimate(
            flops=2 * LANE * LANE * 256 * LANE + 16 * LAG_ROWS * 1024 * 256,
            transcendentals=0,
            bytes_accessed=7 * 1024 * 1024,
        ),
        name="correlate",
    )(place, row_blocks, *col_blocks, table)


def finish_kernel(member_ref, *refs):
    parts, order_ref, out_ref, buf = refs[:8], refs[8], refs[9], refs[10]
    z = member_ref[0] // 16
    pair = pl.program_id(0)
    at = pl.multiple_of(pair % 2 * LANE, LANE)
    for half in range(2):
        for far in range(2):
            wide = jnp.concatenate(
                [p[pair // 2, :, pl.ds(at, LANE)] for p in parts[far * 4 : far * 4 + 4]], 1
            )
            ordered = jnp.dot(wide, order_ref[far, half], preferred_element_type=jnp.float32)
            tile = z ^ far
            for r in range(2):
                buf[pl.ds(half * 4 * LAGS + tile * 2 + r, LAGS, stride=4), :] = ordered[
                    :LAGS, r * LANE : (r + 1) * LANE
                ]
    out_ref[0] = buf[...].astype(jnp.bfloat16)


def finish(member, parts, order):
    whole = pl.BlockSpec(memory_space=pltpu.VMEM)
    return pl.pallas_call(
        finish_kernel,
        grid=(4,),
        in_specs=[pl.BlockSpec(memory_space=pltpu.SMEM)] + [whole] * 9,
        out_specs=pl.BlockSpec((1, 8 * LAGS, LANE), lambda i: (i, 0, 0)),
        out_shape=jax.ShapeDtypeStruct((4, 8 * LAGS, LANE), jnp.bfloat16),
        scratch_shapes=[pltpu.VMEM((8 * LAGS, LANE), jnp.float32)],
        compiler_params=vmem(18),
        name="finish",
    )(member, *parts, order)


def lag_table(zero):
    lag = jnp.arange(LAG_ROWS, dtype=jnp.int32)[:, None] + zero
    k = jnp.arange(2 * BINS, dtype=jnp.int32)[None, :]
    frequency = k % TAPS * LANE + k // 8
    n = frequency * (lag - BINS // 2) + k // TAPS % 2 * (BINS // 2)
    turn = (n + BINS // 4) >> 8
    x = (n - (turn << 8)).astype(jnp.float32) * (math.pi / BINS)
    x2 = x * x
    cos, sin = jnp.float32(0), jnp.float32(0)
    for power in range(10, -1, -2):
        cos = cos * x2 + (-1) ** (power // 2) / math.factorial(power)
        sin = sin * x2 + (-1) ** (power // 2) / math.factorial(power + 1)
    values = jnp.where(turn & 1 == 0, cos, sin * x)
    values = jnp.where((turn + 1) & 2 == 0, values, -values)
    return jnp.where(lag < LAGS, values, 0.0).astype(jnp.bfloat16)


def column_order(member):
    x, y = member // 4 % 4, member % 4
    at = jnp.arange(512, dtype=jnp.int32)
    d, half, e, turn, ch = at // 128, at // 64 % 2, at // 16 % 4, at // 8 % 2, at % 8
    first = (x ^ d) * 32 + (y ^ e) * 8 + ch
    second = (x ^ e) * 32 + (y ^ d) * 8 + ch
    target = jnp.stack([first, second], 0) + (128 * turn + 256 * half)[None]
    column = jnp.arange(256, dtype=jnp.int32)[None, None, None, :]
    side = jnp.arange(2, dtype=jnp.int32)[None, :, None, None]
    return (target[:, None, :, None] == column + 256 * side).astype(jnp.bfloat16)


def on_device(spectra, partners):
    member = lax.axis_index("mem").astype(jnp.int32)
    plane = lax.axis_index("grp").astype(jnp.int32) >> 1
    factor = math.sqrt(2.0 / (BINS * (COMP // 2)))
    white = whiten(spectra)

    row_masks, col_masks = (4, 1), (1, 4)
    members = range(lax.axis_size("mem"))
    lines = [
        [[m ^ (d * mask) for d in range(4)] for m in members if m & (3 * mask) == 0] for mask in row_masks
    ]
    rows = [
        lax.all_gather(white, "mem", axis_index_groups=groups).reshape(4, LANE, CH, LANE)
        for groups in lines
    ]
    places = [(member // mask % 4).reshape(1) for mask in row_masks]
    up, down = ring_perm(white, 1), ring_perm(white, -1)
    member_now, up, down = lax.optimization_barrier((member, up, down))
    tops = [ring_perm(up[: LANE // 2], 1), ring_perm(down[LANE // 2 :], -1)]
    where = jnp.stack([member_now, plane])
    where, up, down, tops = lax.optimization_barrier((where, up, down, tops))

    mine = choose(pick_kernel, "pick", where, partners, [white, down, up, *tops])
    other = xor_perm(mine, "grp", 1)
    near = choose(merge_kernel, "merge", where, partners, [mine, other])
    near, where = lax.optimization_barrier((near, where))
    across = xor_perm(near, "mem", 16)
    hop = xor_perm(near, "mem", 2 * col_masks[1])
    order = column_order(where[0])
    later, order = lax.optimization_barrier((near, order))
    near1, near2, near3 = [xor_perm(later, "mem", e * col_masks[0]) for e in (1, 2, 3)]
    table = lag_table(where[0] - member)
    table, order, hop, across = lax.optimization_barrier((table, order, hop, across))
    far2 = xor_perm(hop, "mem", 16)
    far3 = xor_perm(across, "mem", 3 * col_masks[1])
    across, near1, near2, near3, far2, far3 = lax.optimization_barrier(
        (across, near1, near2, near3, far2, far3)
    )
    far1 = xor_perm(across, "mem", col_masks[1])
    cols = [[near, near1, near2, near3], [across, far1, far2, far3]]
    parts = []
    for n in range(2):
        sums = correlate(places[n], rows[n], cols[n], table, factor)
        parts += [sums[0]] + [xor_perm(sums[d], "mem", d * row_masks[n]) for d in range(1, 4)]
        cols[1], sums = lax.optimization_barrier((cols[1], sums[0]))
    packed = finish(member.reshape(1), parts, order)
    result = packed.reshape(CH, LAGS, 2, 2, LANE)
    return jnp.transpose(result, (0, 3, 2, 4, 1)).reshape(CH, 2, 256, LAGS)


def solution(mesh):
    placed = (P(("grp", "mem"), None, None, None), P())
    return jax.shard_map(
        on_device,
        mesh=mesh,
        in_specs=placed,
        out_specs=P(("grp", "mem"), None, None, None),
        check_vma=False,
    )
```

```python
import math

import jax
import jax.numpy as jnp
from jax import lax
from jax.experimental import pallas as pl
from jax.experimental.pallas import tpu as pltpu
from jax.sharding import PartitionSpec as P

SMOOTH = 32
CH = 8
COMP = 32
BINS = 512
LANE = 128
TAPS = BINS // LANE
LAGS = BINS + 1
LAG_ROWS = 520
UNROLL = 32


def vmem(mib):
    return pltpu.CompilerParams(vmem_limit_bytes=mib * 1024 * 1024)


def xor_perm(array, axis, mask):
    return lax.ppermute(array, axis, [(i, i ^ mask) for i in range(lax.axis_size(axis))])


def whiten_kernel(spectra_ref, out_ref, rows):
    comps = spectra_ref[...].astype(jnp.float32)
    power = (comps[:, 0] * comps[:, 0] + comps[:, 1] * comps[:, 1]).reshape(-1, BINS)
    row = lax.broadcasted_iota(jnp.int32, (BINS, BINS), 0)
    col = lax.broadcasted_iota(jnp.int32, (BINS, BINS), 1)
    band = (jnp.abs(row - col) <= SMOOTH).astype(jnp.float32)
    smooth = jnp.dot(
        power, band, precision=lax.Precision.HIGHEST, preferred_element_type=jnp.float32
    )
    inv = lax.rsqrt(smooth / (2 * SMOOTH + 1) + 1e-05)
    segs = COMP // 2
    for ch in range(CH):
        level = inv[ch * segs : (ch + 1) * segs]
        white = jnp.concatenate([comps[ch, 0] * level, comps[ch, 1] * level], 0)
        taps = jnp.concatenate([white[:, k * LANE : (k + 1) * LANE] for k in range(TAPS)], 0)
        rows[pl.ds(ch, LANE, stride=CH), :] = taps.T
    out_ref[...] = rows[...].reshape(LANE, CH, LANE).astype(jnp.bfloat16)


def whiten(spectra):
    return pl.pallas_call(
        whiten_kernel,
        out_shape=jax.ShapeDtypeStruct((LANE, CH, LANE), jnp.bfloat16),
        scratch_shapes=[pltpu.VMEM((LANE * CH, LANE), jnp.float32)],
        compiler_params=vmem(10),
        name="whiten",
    )(spectra)


def pick_kernel(offsets_ref, *refs):
    planes, out_ref = refs[:4], refs[4]
    for r in range(2):
        for d in range(4):

            @pl.when(offsets_ref[r] >> 1 == d)
            def _():
                out_ref[r] = planes[d][...]


def merge_kernel(offsets_ref, mine_ref, other_ref, out_ref):
    for r in range(2):
        swap = offsets_ref[r] & 1

        @pl.when(swap == 1)
        def _():
            out_ref[r] = other_ref[r]

        @pl.when(swap == 0)
        def _():
            out_ref[r] = mine_ref[r]


def choose(kernel, name, offsets, arrays):
    smem, whole = pl.BlockSpec(memory_space=pltpu.SMEM), pl.BlockSpec(memory_space=pltpu.VMEM)
    return pl.pallas_call(
        kernel,
        in_specs=[smem] + [whole] * len(arrays),
        out_shape=jax.ShapeDtypeStruct((2, LANE, CH, LANE), jnp.bfloat16),
        compiler_params=vmem(10),
        name=name,
    )(offsets, *arrays)


def corr_kernel(factor, *refs):
    row_refs, col_refs, table_ref = refs[:4], refs[4:8], refs[8]
    out_refs, rows, cross = refs[9:13], refs[13], refs[14]
    lane = lax.broadcasted_iota(jnp.int32, (CH * LANE, LANE), 1)
    imag = lane // 16 % 2 == 1
    for d in range(4):
        own = row_refs[d][...].astype(jnp.float32).reshape(CH * LANE, LANE)
        rows[pl.ds(d * 1024, 1024), :] = own
        rows[pl.ds(4096 + d * 1024, 1024), :] = jnp.where(
            imag, -pltpu.roll(own, 16, 1), pltpu.roll(own, LANE - 16, 1)
        )
    sub = lax.broadcasted_iota(jnp.int32, (8, LANE), 0)
    tap = lax.broadcasted_iota(jnp.int32, (8, LANE), 1) // COMP
    pick_re = sub == tap
    pick_im = sub - TAPS == tap
    blank = jnp.zeros((64, LANE), jnp.bfloat16)

    def step(g):
        cols = jnp.concatenate(
            [c[n, g].astype(jnp.float32) for c in col_refs for n in range(2)], 0
        ).astype(jnp.bfloat16)
        rhs = jnp.concatenate(
            [jnp.concatenate([cols, blank], 1), jnp.concatenate([blank, cols], 1)], 0
        )
        pairs = []
        for pair in range(16):
            halves = []
            for half in range(2):
                i = 2 * pair + half
                at = (i // 8) * 1024 + g * 8 + i % 8
                re = rows[pl.ds(at, 8, stride=0), :]
                im = rows[pl.ds(4096 + at, 8, stride=0), :]
                halves.append(jnp.where(pick_re, re, jnp.where(pick_im, im, 0.0)))
            pairs.append(jnp.concatenate(halves, 1))
        lhs = jnp.concatenate(pairs, 0).astype(jnp.bfloat16)
        prod = lax.dot_general(
            lhs, rhs, (((1,), (1,)), ((), ())), preferred_element_type=jnp.float32
        )
        at = pl.multiple_of(g * 8, 8)
        for pair in range(16):
            cross[pair, pl.ds(at, 8), :] = prod[pair * 8 : pair * 8 + 8]

    def steps(k, carry):
        for u in range(UNROLL):
            step(k * UNROLL + u)
        return carry

    lax.fori_loop(0, LANE // UNROLL, steps, 0)
    table = table_ref[...]
    for d in range(4):
        for quad in range(2):
            pair = d * 4 + quad * 2
            weights = jnp.concatenate([cross[pair], cross[pair + 1]], 1).astype(jnp.bfloat16)
            lags = jnp.dot(table, weights, preferred_element_type=jnp.float32)
            out_refs[d][quad] = (lags * factor).astype(jnp.bfloat16)


def correlate(row_blocks, col_blocks, table, factor):
    def body(*refs):
        corr_kernel(factor, *refs)

    return pl.pallas_call(
        body,
        out_shape=[jax.ShapeDtypeStruct((2, LAG_ROWS, 256), jnp.bfloat16)] * 4,
        scratch_shapes=[
            pltpu.VMEM((8 * 1024, LANE), jnp.float32),
            pltpu.VMEM((16, 1024, LANE), jnp.float32),
        ],
        compiler_params=vmem(24),
        cost_estimate=pl.CostEstimate(
            flops=2 * LANE * LANE * 256 * LANE + 16 * LAG_ROWS * 1024 * 256,
            transcendentals=0,
            bytes_accessed=7 * 1024 * 1024,
        ),
        name="correlate",
    )(*row_blocks, *col_blocks, table)


def finish_kernel(member_ref, *refs):
    parts, order_ref, out_ref, buf = refs[:8], refs[8], refs[9], refs[10]
    z = member_ref[0] // 16
    pair = pl.program_id(0)
    at = pl.multiple_of(pair % 2 * LANE, LANE)
    for half in range(2):
        for far in range(2):
            wide = jnp.concatenate(
                [p[pair // 2, :, pl.ds(at, LANE)] for p in parts[far * 4 : far * 4 + 4]], 1
            )
            ordered = jnp.dot(wide, order_ref[far, half], preferred_element_type=jnp.float32)
            tile = z ^ far
            for r in range(2):
                buf[pl.ds(half * 4 * LAGS + tile * 2 + r, LAGS, stride=4), :] = ordered[
                    :LAGS, r * LANE : (r + 1) * LANE
                ]
    out_ref[0] = buf[...].astype(jnp.bfloat16)


def finish(member, parts, order):
    whole = pl.BlockSpec(memory_space=pltpu.VMEM)
    return pl.pallas_call(
        finish_kernel,
        grid=(4,),
        in_specs=[pl.BlockSpec(memory_space=pltpu.SMEM)] + [whole] * 9,
        out_specs=pl.BlockSpec((1, 8 * LAGS, LANE), lambda i: (i, 0, 0)),
        out_shape=jax.ShapeDtypeStruct((4, 8 * LAGS, LANE), jnp.bfloat16),
        scratch_shapes=[pltpu.VMEM((8 * LAGS, LANE), jnp.float32)],
        compiler_params=vmem(18),
        name="finish",
    )(member, *parts, order)


def lag_table():
    lag = jnp.arange(LAG_ROWS, dtype=jnp.int32)[:, None]
    k = jnp.arange(2 * BINS, dtype=jnp.int32)[None, :]
    frequency = k % TAPS * LANE + k // 8
    n = frequency * (lag - BINS // 2) + k // TAPS % 2 * (BINS // 2)
    turn = (n + BINS // 4) >> 8
    x = (n - (turn << 8)).astype(jnp.float32) * (math.pi / BINS)
    x2 = x * x
    cos, sin = jnp.float32(0), jnp.float32(0)
    for power in range(10, -1, -2):
        cos = cos * x2 + (-1) ** (power // 2) / math.factorial(power)
        sin = sin * x2 + (-1) ** (power // 2) / math.factorial(power + 1)
    values = jnp.where(turn & 1 == 0, cos, sin * x)
    values = jnp.where((turn + 1) & 2 == 0, values, -values)
    return jnp.where(lag < LAGS, values, 0.0).astype(jnp.bfloat16)


def column_order(member):
    x, y = member // 4 % 4, member % 4
    at = jnp.arange(512, dtype=jnp.int32)
    d, half, e, turn, ch = at // 128, at // 64 % 2, at // 16 % 4, at // 8 % 2, at % 8
    first = (x ^ d) * 32 + (y ^ e) * 8 + ch
    second = (x ^ e) * 32 + (y ^ d) * 8 + ch
    target = jnp.stack([first, second], 0) + (128 * turn + 256 * half)[None]
    column = jnp.arange(256, dtype=jnp.int32)[None, None, None, :]
    side = jnp.arange(2, dtype=jnp.int32)[None, :, None, None]
    return (target[:, None, :, None] == column + 256 * side).astype(jnp.bfloat16)


def on_device(spectra, partners):
    member = lax.axis_index("mem").astype(jnp.int32)
    factor = math.sqrt(2.0 / (BINS * (COMP // 2)))
    white = whiten(spectra)

    row_masks, col_masks = (4, 1), (1, 4)
    rows = [[white, None, None, None], [white, None, None, None]]

    plane1, plane2, plane3 = [xor_perm(white, "grp", 2 * d) for d in (1, 2, 3)]
    source = white
    for d in (1, 3, 2):
        sent = [xor_perm(source, "mem", d * mask) for mask in row_masks]
        source, sent = lax.optimization_barrier((source, sent))
        rows[0][d], rows[1][d] = sent
    offsets = lax.dynamic_index_in_dim(partners, member, 1, keepdims=False)
    table = lag_table()
    table, rows, offsets, white, plane1, plane3, plane2 = lax.optimization_barrier(
        (table, rows, offsets, white, plane1, plane3, plane2)
    )

    mine = choose(pick_kernel, "pick", offsets, [white, plane1, plane2, plane3])
    other = xor_perm(mine, "grp", 1)
    near = choose(merge_kernel, "merge", offsets, [mine, other])
    near, member_now = lax.optimization_barrier((near, member))
    across = xor_perm(near, "mem", 16)
    hop = xor_perm(near, "mem", 2 * col_masks[1])
    order = column_order(member_now)
    later, order = lax.optimization_barrier((near, order))
    near1, near2, near3 = [xor_perm(later, "mem", e * col_masks[0]) for e in (1, 2, 3)]
    order, hop, across = lax.optimization_barrier((order, hop, across))
    far2 = xor_perm(hop, "mem", 16)
    far3 = xor_perm(across, "mem", 3 * col_masks[1])
    across, near1, near2, near3, far2, far3 = lax.optimization_barrier(
        (across, near1, near2, near3, far2, far3)
    )
    far1 = xor_perm(across, "mem", col_masks[1])
    cols = [[near, near1, near2, near3], [across, far1, far2, far3]]
    parts = []
    for n in range(2):
        sums = correlate(rows[n], cols[n], table, factor)
        parts += [sums[0]] + [xor_perm(sums[d], "mem", d * row_masks[n]) for d in range(1, 4)]
        cols[1], sums = lax.optimization_barrier((cols[1], sums[0]))
    packed = finish(member.reshape(1), parts, order)
    result = packed.reshape(CH, LAGS, 2, 2, LANE)
    return jnp.transpose(result, (0, 3, 2, 4, 1)).reshape(CH, 2, 256, LAGS)


def solution(mesh):
    placed = (P(("grp", "mem"), None, None, None), P())
    return jax.shard_map(
        on_device,
        mesh=mesh,
        in_specs=placed,
        out_specs=P(("grp", "mem"), None, None, None),
        check_vma=False,
    )
```

```python
import math

import jax
import jax.numpy as jnp
from jax import lax
from jax.experimental import pallas as pl
from jax.experimental.pallas import tpu as pltpu
from jax.sharding import PartitionSpec as P

SMOOTH = 32
CH = 8
COMP = 32
BINS = 512
LANE = 128
TAPS = BINS // LANE
LAGS = BINS + 1
LAG_ROWS = 520
UNROLL = 32


def vmem(mib):
    return pltpu.CompilerParams(vmem_limit_bytes=mib * 1024 * 1024)


def xor_perm(array, axis, mask):
    return lax.ppermute(array, axis, [(i, i ^ mask) for i in range(lax.axis_size(axis))])


def whiten_kernel(spectra_ref, out_ref, rows):
    comps = spectra_ref[...].astype(jnp.float32)
    power = (comps[:, 0] * comps[:, 0] + comps[:, 1] * comps[:, 1]).reshape(-1, BINS)
    row = lax.broadcasted_iota(jnp.int32, (BINS, BINS), 0)
    col = lax.broadcasted_iota(jnp.int32, (BINS, BINS), 1)
    band = (jnp.abs(row - col) <= SMOOTH).astype(jnp.float32)
    smooth = jnp.dot(
        power, band, precision=lax.Precision.HIGHEST, preferred_element_type=jnp.float32
    )
    inv = lax.rsqrt(smooth / (2 * SMOOTH + 1) + 1e-05)
    segs = COMP // 2
    for ch in range(CH):
        level = inv[ch * segs : (ch + 1) * segs]
        white = jnp.concatenate([comps[ch, 0] * level, comps[ch, 1] * level], 0)
        taps = jnp.concatenate([white[:, k * LANE : (k + 1) * LANE] for k in range(TAPS)], 0)
        rows[pl.ds(ch, LANE, stride=CH), :] = taps.T
    out_ref[...] = rows[...].reshape(LANE, CH, LANE).astype(jnp.bfloat16)


def whiten(spectra):
    return pl.pallas_call(
        whiten_kernel,
        out_shape=jax.ShapeDtypeStruct((LANE, CH, LANE), jnp.bfloat16),
        scratch_shapes=[pltpu.VMEM((LANE * CH, LANE), jnp.float32)],
        compiler_params=vmem(10),
        name="whiten",
    )(spectra)


def pick_kernel(offsets_ref, *refs):
    planes, out_ref = refs[:4], refs[4]
    for r in range(2):
        for d in range(4):

            @pl.when(offsets_ref[r] >> 1 == d)
            def _():
                out_ref[r] = planes[d][...]


def merge_kernel(offsets_ref, mine_ref, other_ref, out_ref):
    for r in range(2):
        swap = offsets_ref[r] & 1

        @pl.when(swap == 1)
        def _():
            out_ref[r] = other_ref[r]

        @pl.when(swap == 0)
        def _():
            out_ref[r] = mine_ref[r]


def choose(kernel, name, offsets, arrays):
    smem, whole = pl.BlockSpec(memory_space=pltpu.SMEM), pl.BlockSpec(memory_space=pltpu.VMEM)
    return pl.pallas_call(
        kernel,
        in_specs=[smem] + [whole] * len(arrays),
        out_shape=jax.ShapeDtypeStruct((2, LANE, CH, LANE), jnp.bfloat16),
        compiler_params=vmem(10),
        name=name,
    )(offsets, *arrays)


def corr_kernel(factor, *refs):
    row_refs, col_refs, table_ref = refs[:4], refs[4:8], refs[8]
    out_refs, rows, cross = refs[9:13], refs[13], refs[14]
    lane = lax.broadcasted_iota(jnp.int32, (CH * LANE, LANE), 1)
    imag = lane // 16 % 2 == 1
    for d in range(4):
        own = row_refs[d][...].astype(jnp.float32).reshape(CH * LANE, LANE)
        rows[pl.ds(d * 1024, 1024), :] = own
        rows[pl.ds(4096 + d * 1024, 1024), :] = jnp.where(
            imag, -pltpu.roll(own, 16, 1), pltpu.roll(own, LANE - 16, 1)
        )
    sub = lax.broadcasted_iota(jnp.int32, (8, LANE), 0)
    tap = lax.broadcasted_iota(jnp.int32, (8, LANE), 1) // COMP
    pick_re = sub == tap
    pick_im = sub - TAPS == tap
    blank = jnp.zeros((64, LANE), jnp.bfloat16)

    def step(g):
        cols = jnp.concatenate(
            [c[n, g].astype(jnp.float32) for c in col_refs for n in range(2)], 0
        ).astype(jnp.bfloat16)
        rhs = jnp.concatenate(
            [jnp.concatenate([cols, blank], 1), jnp.concatenate([blank, cols], 1)], 0
        )
        pairs = []
        for pair in range(16):
            halves = []
            for half in range(2):
                i = 2 * pair + half
                at = (i // 8) * 1024 + g * 8 + i % 8
                re = rows[pl.ds(at, 8, stride=0), :]
                im = rows[pl.ds(4096 + at, 8, stride=0), :]
                halves.append(jnp.where(pick_re, re, jnp.where(pick_im, im, 0.0)))
            pairs.append(jnp.concatenate(halves, 1))
        lhs = jnp.concatenate(pairs, 0).astype(jnp.bfloat16)
        prod = lax.dot_general(
            lhs, rhs, (((1,), (1,)), ((), ())), preferred_element_type=jnp.float32
        )
        at = pl.multiple_of(g * 8, 8)
        for pair in range(16):
            cross[pair, pl.ds(at, 8), :] = prod[pair * 8 : pair * 8 + 8]

    def steps(k, carry):
        for u in range(UNROLL):
            step(k * UNROLL + u)
        return carry

    lax.fori_loop(0, LANE // UNROLL, steps, 0)
    table = table_ref[...]
    for d in range(4):
        for quad in range(2):
            pair = d * 4 + quad * 2
            weights = jnp.concatenate([cross[pair], cross[pair + 1]], 1).astype(jnp.bfloat16)
            lags = jnp.dot(table, weights, preferred_element_type=jnp.float32)
            out_refs[d][quad] = (lags * factor).astype(jnp.bfloat16)


def correlate(row_blocks, col_blocks, table, factor):
    def body(*refs):
        corr_kernel(factor, *refs)

    return pl.pallas_call(
        body,
        out_shape=[jax.ShapeDtypeStruct((2, LAG_ROWS, 256), jnp.bfloat16)] * 4,
        scratch_shapes=[
            pltpu.VMEM((8 * 1024, LANE), jnp.float32),
            pltpu.VMEM((16, 1024, LANE), jnp.float32),
        ],
        compiler_params=vmem(24),
        cost_estimate=pl.CostEstimate(
            flops=2 * LANE * LANE * 256 * LANE + 16 * LAG_ROWS * 1024 * 256,
            transcendentals=0,
            bytes_accessed=7 * 1024 * 1024,
        ),
        name="correlate",
    )(*row_blocks, *col_blocks, table)


def finish_kernel(member_ref, *refs):
    parts, order_ref, out_ref, buf = refs[:8], refs[8], refs[9], refs[10]
    z = member_ref[0] // 16
    pair = pl.program_id(0)
    at = pl.multiple_of(pair % 2 * LANE, LANE)
    for half in range(2):
        for far in range(2):
            wide = jnp.concatenate(
                [p[pair // 2, :, pl.ds(at, LANE)] for p in parts[far * 4 : far * 4 + 4]], 1
            )
            ordered = jnp.dot(wide, order_ref[far, half], preferred_element_type=jnp.float32)
            tile = z ^ far
            for r in range(2):
                buf[pl.ds(half * 4 * LAGS + tile * 2 + r, LAGS, stride=4), :] = ordered[
                    :LAGS, r * LANE : (r + 1) * LANE
                ]
    out_ref[0] = buf[...].astype(jnp.bfloat16)


def finish(member, parts, order):
    whole = pl.BlockSpec(memory_space=pltpu.VMEM)
    return pl.pallas_call(
        finish_kernel,
        grid=(4,),
        in_specs=[pl.BlockSpec(memory_space=pltpu.SMEM)] + [whole] * 9,
        out_specs=pl.BlockSpec((1, 8 * LAGS, LANE), lambda i: (i, 0, 0)),
        out_shape=jax.ShapeDtypeStruct((4, 8 * LAGS, LANE), jnp.bfloat16),
        scratch_shapes=[pltpu.VMEM((8 * LAGS, LANE), jnp.float32)],
        compiler_params=vmem(18),
        name="finish",
    )(member, *parts, order)


def lag_table():
    lag = jnp.arange(LAG_ROWS, dtype=jnp.int32)[:, None]
    k = jnp.arange(2 * BINS, dtype=jnp.int32)[None, :]
    frequency = k % TAPS * LANE + k // 8
    n = frequency * (lag - BINS // 2) + k // TAPS % 2 * (BINS // 2)
    turn = (n + BINS // 4) >> 8
    x = (n - (turn << 8)).astype(jnp.float32) * (math.pi / BINS)
    x2 = x * x
    cos, sin = jnp.float32(0), jnp.float32(0)
    for power in range(10, -1, -2):
        cos = cos * x2 + (-1) ** (power // 2) / math.factorial(power)
        sin = sin * x2 + (-1) ** (power // 2) / math.factorial(power + 1)
    values = jnp.where(turn & 1 == 0, cos, sin * x)
    values = jnp.where((turn + 1) & 2 == 0, values, -values)
    return jnp.where(lag < LAGS, values, 0.0).astype(jnp.bfloat16)


def column_order(member):
    x, y = member // 4 % 4, member % 4
    at = jnp.arange(512, dtype=jnp.int32)
    d, half, e, turn, ch = at // 128, at // 64 % 2, at // 16 % 4, at // 8 % 2, at % 8
    first = (x ^ d) * 32 + (y ^ e) * 8 + ch
    second = (x ^ e) * 32 + (y ^ d) * 8 + ch
    target = jnp.stack([first, second], 0) + (128 * turn + 256 * half)[None]
    column = jnp.arange(256, dtype=jnp.int32)[None, None, None, :]
    side = jnp.arange(2, dtype=jnp.int32)[None, :, None, None]
    return (target[:, None, :, None] == column + 256 * side).astype(jnp.bfloat16)


def on_device(spectra, partners):
    member = lax.axis_index("mem").astype(jnp.int32)
    factor = math.sqrt(2.0 / (BINS * (COMP // 2)))
    white = whiten(spectra)

    row_masks, col_masks = (4, 1), (1, 4)
    rows = [[white, None, None, None], [white, None, None, None]]

    plane1, plane2, plane3 = [xor_perm(white, "grp", 2 * d) for d in (1, 2, 3)]
    source = white
    for d in (1, 3, 2):
        sent = [xor_perm(source, "mem", d * mask) for mask in row_masks]
        source, sent = lax.optimization_barrier((source, sent))
        rows[0][d], rows[1][d] = sent
    offsets = lax.dynamic_index_in_dim(partners, member, 1, keepdims=False)
    table = lag_table()
    table, rows, offsets, white, plane1, plane3, plane2 = lax.optimization_barrier(
        (table, rows, offsets, white, plane1, plane3, plane2)
    )

    mine = choose(pick_kernel, "pick", offsets, [white, plane1, plane2, plane3])
    other = xor_perm(mine, "grp", 1)
    near = choose(merge_kernel, "merge", offsets, [mine, other])
    near, member_now = lax.optimization_barrier((near, member))
    across = xor_perm(near, "mem", 16)
    hop = xor_perm(near, "mem", 2 * col_masks[1])
    order = column_order(member_now)
    near1, near2, near3 = [xor_perm(near, "mem", e * col_masks[0]) for e in (1, 2, 3)]
    order, hop, across = lax.optimization_barrier((order, hop, across))
    far2 = xor_perm(hop, "mem", 16)
    far3 = xor_perm(across, "mem", 3 * col_masks[1])
    across, near1, near2, near3 = lax.optimization_barrier((across, near1, near2, near3))
    far1 = xor_perm(across, "mem", col_masks[1])
    cols = [[near, near1, near2, near3], [across, far1, far2, far3]]
    parts = []
    for n in range(2):
        sums = correlate(rows[n], cols[n], table, factor)
        parts += [sums[0]] + [xor_perm(sums[d], "mem", d * row_masks[n]) for d in range(1, 4)]
        cols[1], sums = lax.optimization_barrier((cols[1], sums[0]))
    packed = finish(member.reshape(1), parts, order)
    result = packed.reshape(CH, LAGS, 2, 2, LANE)
    return jnp.transpose(result, (0, 3, 2, 4, 1)).reshape(CH, 2, 256, LAGS)


def solution(mesh):
    placed = (P(("grp", "mem"), None, None, None), P())
    return jax.shard_map(
        on_device,
        mesh=mesh,
        in_specs=placed,
        out_specs=P(("grp", "mem"), None, None, None),
        check_vma=False,
    )
```

```python
import math

import jax
import jax.numpy as jnp
from jax import lax
from jax.experimental import pallas as pl
from jax.experimental.pallas import tpu as pltpu
from jax.sharding import PartitionSpec as P

SMOOTH = 32
CH = 8
COMP = 32
BINS = 512
LANE = 128
TAPS = BINS // LANE
LAGS = BINS + 1
LAG_ROWS = 520
UNROLL = 32


def vmem(mib):
    return pltpu.CompilerParams(vmem_limit_bytes=mib * 1024 * 1024)


def xor_perm(array, axis, mask):
    return lax.ppermute(array, axis, [(i, i ^ mask) for i in range(lax.axis_size(axis))])


def whiten_kernel(spectra_ref, out_ref, rows):
    comps = spectra_ref[...].astype(jnp.float32)
    power = (comps[:, 0] * comps[:, 0] + comps[:, 1] * comps[:, 1]).reshape(-1, BINS)
    row = lax.broadcasted_iota(jnp.int32, (BINS, BINS), 0)
    col = lax.broadcasted_iota(jnp.int32, (BINS, BINS), 1)
    band = (jnp.abs(row - col) <= SMOOTH).astype(jnp.float32)
    smooth = jnp.dot(
        power, band, precision=lax.Precision.HIGHEST, preferred_element_type=jnp.float32
    )
    inv = lax.rsqrt(smooth / (2 * SMOOTH + 1) + 1e-05)
    segs = COMP // 2
    for ch in range(CH):
        level = inv[ch * segs : (ch + 1) * segs]
        white = jnp.concatenate([comps[ch, 0] * level, comps[ch, 1] * level], 0)
        taps = jnp.concatenate([white[:, k * LANE : (k + 1) * LANE] for k in range(TAPS)], 0)
        rows[pl.ds(ch, LANE, stride=CH), :] = taps.T
    out_ref[...] = rows[...].reshape(LANE, CH, LANE).astype(jnp.bfloat16)


def whiten(spectra):
    return pl.pallas_call(
        whiten_kernel,
        out_shape=jax.ShapeDtypeStruct((LANE, CH, LANE), jnp.bfloat16),
        scratch_shapes=[pltpu.VMEM((LANE * CH, LANE), jnp.float32)],
        compiler_params=vmem(10),
        name="whiten",
    )(spectra)


def pick_kernel(offsets_ref, *refs):
    planes, out_ref = refs[:4], refs[4]
    for r in range(2):
        for d in range(4):

            @pl.when(offsets_ref[r] >> 1 == d)
            def _():
                out_ref[r] = planes[d][...]


def merge_kernel(offsets_ref, mine_ref, other_ref, out_ref):
    for r in range(2):
        swap = offsets_ref[r] & 1

        @pl.when(swap == 1)
        def _():
            out_ref[r] = other_ref[r]

        @pl.when(swap == 0)
        def _():
            out_ref[r] = mine_ref[r]


def choose(kernel, name, offsets, arrays):
    smem, whole = pl.BlockSpec(memory_space=pltpu.SMEM), pl.BlockSpec(memory_space=pltpu.VMEM)
    return pl.pallas_call(
        kernel,
        in_specs=[smem] + [whole] * len(arrays),
        out_shape=jax.ShapeDtypeStruct((2, LANE, CH, LANE), jnp.bfloat16),
        compiler_params=vmem(10),
        name=name,
    )(offsets, *arrays)


def hold(blocks):
    def body(*refs):
        for n in range(3):
            refs[3 + n][...] = refs[n][...]

    return pl.pallas_call(
        body,
        out_shape=[jax.ShapeDtypeStruct((LANE, CH, LANE), jnp.bfloat16)] * 3,
        compiler_params=vmem(6),
        name="hold",
    )(*blocks)


def corr_kernel(factor, *refs):
    row_refs, col_refs, table_ref = refs[:4], refs[4:8], refs[8]
    out_refs, rows, cross = refs[9:13], refs[13], refs[14]
    lane = lax.broadcasted_iota(jnp.int32, (CH * LANE, LANE), 1)
    imag = lane // 16 % 2 == 1
    for d in range(4):
        own = row_refs[d][...].astype(jnp.float32).reshape(CH * LANE, LANE)
        rows[pl.ds(d * 1024, 1024), :] = own
        rows[pl.ds(4096 + d * 1024, 1024), :] = jnp.where(
            imag, -pltpu.roll(own, 16, 1), pltpu.roll(own, LANE - 16, 1)
        )
    sub = lax.broadcasted_iota(jnp.int32, (8, LANE), 0)
    tap = lax.broadcasted_iota(jnp.int32, (8, LANE), 1) // COMP
    pick_re = sub == tap
    pick_im = sub - TAPS == tap
    blank = jnp.zeros((64, LANE), jnp.bfloat16)

    def step(g):
        cols = jnp.concatenate(
            [c[n, g].astype(jnp.float32) for c in col_refs for n in range(2)], 0
        ).astype(jnp.bfloat16)
        rhs = jnp.concatenate(
            [jnp.concatenate([cols, blank], 1), jnp.concatenate([blank, cols], 1)], 0
        )
        pairs = []
        for pair in range(16):
            halves = []
            for half in range(2):
                i = 2 * pair + half
                at = (i // 8) * 1024 + g * 8 + i % 8
                re = rows[pl.ds(at, 8, stride=0), :]
                im = rows[pl.ds(4096 + at, 8, stride=0), :]
                halves.append(jnp.where(pick_re, re, jnp.where(pick_im, im, 0.0)))
            pairs.append(jnp.concatenate(halves, 1))
        lhs = jnp.concatenate(pairs, 0).astype(jnp.bfloat16)
        prod = lax.dot_general(
            lhs, rhs, (((1,), (1,)), ((), ())), preferred_element_type=jnp.float32
        )
        at = pl.multiple_of(g * 8, 8)
        for pair in range(16):
            cross[pair, pl.ds(at, 8), :] = prod[pair * 8 : pair * 8 + 8]

    def steps(k, carry):
        for u in range(UNROLL):
            step(k * UNROLL + u)
        return carry

    lax.fori_loop(0, LANE // UNROLL, steps, 0)
    table = table_ref[...]
    for d in range(4):
        for quad in range(2):
            pair = d * 4 + quad * 2
            weights = jnp.concatenate([cross[pair], cross[pair + 1]], 1).astype(jnp.bfloat16)
            lags = jnp.dot(table, weights, preferred_element_type=jnp.float32)
            out_refs[d][quad] = (lags * factor).astype(jnp.bfloat16)


def correlate(row_blocks, col_blocks, table, factor):
    def body(*refs):
        corr_kernel(factor, *refs)

    return pl.pallas_call(
        body,
        out_shape=[jax.ShapeDtypeStruct((2, LAG_ROWS, 256), jnp.bfloat16)] * 4,
        scratch_shapes=[
            pltpu.VMEM((8 * 1024, LANE), jnp.float32),
            pltpu.VMEM((16, 1024, LANE), jnp.float32),
        ],
        compiler_params=vmem(24),
        cost_estimate=pl.CostEstimate(
            flops=2 * LANE * LANE * 256 * LANE + 16 * LAG_ROWS * 1024 * 256,
            transcendentals=0,
            bytes_accessed=7 * 1024 * 1024,
        ),
        name="correlate",
    )(*row_blocks, *col_blocks, table)


def finish_kernel(member_ref, *refs):
    parts, order_ref, out_ref, buf = refs[:8], refs[8], refs[9], refs[10]
    z = member_ref[0] // 16
    pair = pl.program_id(0)
    at = pl.multiple_of(pair % 2 * LANE, LANE)
    for half in range(2):
        for far in range(2):
            wide = jnp.concatenate(
                [p[pair // 2, :, pl.ds(at, LANE)] for p in parts[far * 4 : far * 4 + 4]], 1
            )
            ordered = jnp.dot(wide, order_ref[far, half], preferred_element_type=jnp.float32)
            tile = z ^ far
            for r in range(2):
                buf[pl.ds(half * 4 * LAGS + tile * 2 + r, LAGS, stride=4), :] = ordered[
                    :LAGS, r * LANE : (r + 1) * LANE
                ]
    out_ref[0] = buf[...].astype(jnp.bfloat16)


def finish(member, parts, order):
    whole = pl.BlockSpec(memory_space=pltpu.VMEM)
    return pl.pallas_call(
        finish_kernel,
        grid=(4,),
        in_specs=[pl.BlockSpec(memory_space=pltpu.SMEM)] + [whole] * 9,
        out_specs=pl.BlockSpec((1, 8 * LAGS, LANE), lambda i: (i, 0, 0)),
        out_shape=jax.ShapeDtypeStruct((4, 8 * LAGS, LANE), jnp.bfloat16),
        scratch_shapes=[pltpu.VMEM((8 * LAGS, LANE), jnp.float32)],
        compiler_params=vmem(18),
        name="finish",
    )(member, *parts, order)


def lag_table():
    lag = jnp.arange(LAG_ROWS, dtype=jnp.int32)[:, None]
    k = jnp.arange(2 * BINS, dtype=jnp.int32)[None, :]
    frequency = k % TAPS * LANE + k // 8
    n = frequency * (lag - BINS // 2) + k // TAPS % 2 * (BINS // 2)
    turn = (n + BINS // 4) >> 8
    x = (n - (turn << 8)).astype(jnp.float32) * (math.pi / BINS)
    x2 = x * x
    cos, sin = jnp.float32(0), jnp.float32(0)
    for power in range(10, -1, -2):
        cos = cos * x2 + (-1) ** (power // 2) / math.factorial(power)
        sin = sin * x2 + (-1) ** (power // 2) / math.factorial(power + 1)
    values = jnp.where(turn & 1 == 0, cos, sin * x)
    values = jnp.where((turn + 1) & 2 == 0, values, -values)
    return jnp.where(lag < LAGS, values, 0.0).astype(jnp.bfloat16)


def column_order(member):
    x, y = member // 4 % 4, member % 4
    at = jnp.arange(512, dtype=jnp.int32)
    d, half, e, turn, ch = at // 128, at // 64 % 2, at // 16 % 4, at // 8 % 2, at % 8
    first = (x ^ d) * 32 + (y ^ e) * 8 + ch
    second = (x ^ e) * 32 + (y ^ d) * 8 + ch
    target = jnp.stack([first, second], 0) + (128 * turn + 256 * half)[None]
    column = jnp.arange(256, dtype=jnp.int32)[None, None, None, :]
    side = jnp.arange(2, dtype=jnp.int32)[None, :, None, None]
    return (target[:, None, :, None] == column + 256 * side).astype(jnp.bfloat16)


def on_device(spectra, partners):
    member = lax.axis_index("mem").astype(jnp.int32)
    factor = math.sqrt(2.0 / (BINS * (COMP // 2)))
    white = whiten(spectra)

    row_masks, col_masks = (4, 1), (1, 4)
    rows = [[white, None, None, None], [white, None, None, None]]

    plane1, plane2, plane3 = [xor_perm(white, "grp", 2 * d) for d in (1, 2, 3)]
    source = white
    for d in (1, 3, 2):
        sent = [xor_perm(source, "mem", d * mask) for mask in row_masks]
        source, sent = lax.optimization_barrier((source, sent))
        rows[0][d], rows[1][d] = sent
    offsets = lax.dynamic_index_in_dim(partners, member, 1, keepdims=False)
    table = lag_table()
    table, rows, offsets, white, plane1, plane3, plane2 = lax.optimization_barrier(
        (table, rows, offsets, white, plane1, plane3, plane2)
    )

    mine = choose(pick_kernel, "pick", offsets, [white, plane1, plane2, plane3])
    other = xor_perm(mine, "grp", 1)
    near = choose(merge_kernel, "merge", offsets, [mine, other])
    near, member_now, kept = lax.optimization_barrier((near, member, rows[0][1:]))
    kept = hold(kept)
    across = xor_perm(near, "mem", 16)
    hop = xor_perm(near, "mem", 2 * col_masks[1])
    order = column_order(member_now)
    near1, near2, near3 = [xor_perm(near, "mem", e * col_masks[0]) for e in (1, 2, 3)]
    kept, order, hop, across = lax.optimization_barrier((kept, order, hop, across))
    rows[0][1:] = kept
    far2 = xor_perm(hop, "mem", 16)
    far3 = xor_perm(across, "mem", 3 * col_masks[1])
    across, near1, near2, near3 = lax.optimization_barrier((across, near1, near2, near3))
    far1 = xor_perm(across, "mem", col_masks[1])
    cols = [[near, near1, near2, near3], [across, far1, far2, far3]]
    parts = []
    for n in range(2):
        sums = correlate(rows[n], cols[n], table, factor)
        parts += [sums[0]] + [xor_perm(sums[d], "mem", d * row_masks[n]) for d in range(1, 4)]
        cols[1], sums = lax.optimization_barrier((cols[1], sums[0]))
    packed = finish(member.reshape(1), parts, order)
    result = packed.reshape(CH, LAGS, 2, 2, LANE)
    return jnp.transpose(result, (0, 3, 2, 4, 1)).reshape(CH, 2, 256, LAGS)


def solution(mesh):
    placed = (P(("grp", "mem"), None, None, None), P())
    return jax.shard_map(
        on_device,
        mesh=mesh,
        in_specs=placed,
        out_specs=P(("grp", "mem"), None, None, None),
        check_vma=False,
    )
```
